32 devices in a mesh: groups: 2 (over y), samples: 8 (over z, x), section: 1, mp: 2 (over core).
Axes of the slice: x: 2, y: 2, z: 4, core: 2. Of those that a mesh axis runs over, the one named last changes fastest.
Arguments:
- stored_inputs: bfloat16 [1, 16, 128, 2048], P('section', ('groups', 'samples'), None, 'mp'), parts along dimension 1
- top_cotangent: bfloat16 [16, 128, 2048], P(('groups', 'samples'), None, 'mp'), parts along dimension 0, may hold values from -0.375 to 0.375
- layer_weights: bfloat16 [1, 2048, 2048], P('section', 'samples', 'mp'), may hold values from -0.125 to 0.125
- block_layout: int32 [1, 2, 2], P('section'), may hold values 0 or 1
- region_mask: int32 [128], replicated, may hold values from 0 to 1, as said below
- partner_samples: int32 [16], P('groups'), parts along dimension 0, may hold values from 0 to 7, as said below
- spins: int32 [16, 128], P(('groups', 'samples')), parts along dimension 0, may hold values from 0 to 1
Outputs:
- weight_grad: float32 [2, 2048, 2048], P(('groups', 'section'), 'samples', 'mp'), parts along dimension 0
- layer_cotangents: bfloat16 [1, 16, 128, 2048], P('section', ('groups', 'samples'), None, 'mp'), parts along dimension 1
- embed_grad: float32 [4, 2048], P('groups', 'mp'), parts along dimension 0
The draws below stay inside these ranges and needn't reach their ends.
There are 2 independent parts, one for each index of `groups`. The reference program is written for one: setup_inputs(seed, part) draws one part's arguments, and reference() takes and returns one part's arrays. A program takes and returns all parts, laid end to end along the dimension named above; an argument that names none is the same for every part. Nothing has to cross between parts.
Inputs may be any that keep to these rules, and one draw needn't show every extreme that they name: `region_mask`: exactly 64 of the 128 entries are 1, the others 0. The samples pair up: partner_samples[partner_samples[r]] = r and partner_samples[r] != r for every sample r. `block_layout`: a query block always sees its own block, whatever the diagonal entry holds.
All inputs are finite; a program needn't handle non-finite values.
Results may differ from the reference program's by a relative error of at most 0.03.
Values may be sent and summed in bfloat16 or wider, within the bound.
A program may use at most 64 MiB of HBM per device.

```python
import jax
import jax.numpy as jnp
from jax import lax

D = 2048
HEAD = 128
BLOCK = 64
SEQ = 128
SPINS = 2
MB = 1
LAYERS = 1
SHARDS = 8
SAMPLES = 8
NB = 2
NA = 64


def draw_stored_inputs(key, part):
    first_key = jax.random.fold_in(key, 0)
    shape = (LAYERS, SAMPLES, SEQ, D)
    return jnp.clip(jax.random.normal(first_key, shape, jnp.float32), -6.0, 6.0).astype(jnp.bfloat16)


def draw_region_mask(key, part):
    order = jax.random.permutation(key, SEQ)
    return jnp.zeros((SEQ,), jnp.int32).at[order[:NA]].set(1)


def draw_partner_samples(key, part):
    shard_key, slot_key, other_key, order_key = jax.random.split(jax.random.fold_in(key, 7), 4)
    shard = jax.random.randint(shard_key, (), 0, SHARDS, dtype=jnp.int32)
    slot_first = jax.random.randint(slot_key, (), 0, MB, dtype=jnp.int32)
    slot_second = jax.random.randint(other_key, (), 0, MB, dtype=jnp.int32)
    first = (shard * MB + slot_first).astype(jnp.int32)
    second = ((shard + SHARDS - 1) % SHARDS * MB + slot_second).astype(jnp.int32)
    scores = jax.random.permutation(order_key, SAMPLES).astype(jnp.int32)
    scores = scores.at[first].set(-2).at[second].set(-1)
    order = jnp.argsort(scores, stable=True).astype(jnp.int32)
    firsts = order[0::2]
    seconds = order[1::2]
    swap_partner = jnp.zeros((SAMPLES,), jnp.int32).at[firsts].set(seconds).at[seconds].set(firsts)
    return swap_partner.astype(jnp.int32)


def touch_ends(values, key, least, top_value):
    extent = values.shape
    place = [jax.random.randint(jax.random.fold_in(key, axis), (), 0, extent[axis]) for axis in range(len(extent))]
    values = values.at[tuple(place)].set(least)
    longest = extent.index(max(extent))
    place[longest] = (place[longest] + 1) % extent[longest]
    return values.at[tuple(place)].set(top_value)


def strengthened(entries, own_key, source, target, parts, factor):
    def block_of(dim):
        return (jnp.arange(entries.shape[dim]) // (entries.shape[dim] // parts)).reshape((-1,) + (1,) * (entries.ndim - 1 - dim))

    near = jax.random.permutation(own_key, parts)[block_of(target)]
    far = (block_of(target) + parts // 2) % parts
    return jnp.where((block_of(source) == near) | (block_of(source) == far), factor * entries, entries)


def level_of(key, dims, cuts, least, high):
    factor_of = 1.0
    for position, parts in cuts:
        draws = jax.random.uniform(jax.random.fold_in(jax.random.fold_in(key, 6), position), (parts,), jnp.float32, least / len(cuts), high / len(cuts))
        factor_of = factor_of * jnp.repeat(jnp.exp(draws), dims[position] // parts).reshape((-1,) + (1,) * (len(dims) - 1 - position))
    return factor_of


def bell_draw(own_key, shape, scale, bound, pieces=(), kind=jnp.bfloat16):
    entries = jax.random.normal(own_key, shape, jnp.float32) * scale
    if len(pieces) > 0:
        entries = level_of(own_key, shape, pieces, -0.22, 0.18) * entries
    return jnp.clip(entries, min=-bound, max=bound).astype(kind)


def bell_draw_with(key, shape, width, most, cuts, heavy, kind=jnp.bfloat16):
    result = width * jax.random.normal(key, shape, jnp.float32)
    if cuts:
        result = result * level_of(key, shape, cuts, -0.22, 0.18)
    return jnp.clip(strengthened(result, jax.random.fold_in(key, 3), *heavy), -most, most).astype(kind)


def setup_inputs(seed: int = 0, part: int = 0) -> dict:
    splits = jax.random.split(jax.random.key(seed), 8)
    part_splits = jax.random.split(jax.random.fold_in(splits[7], part), 8)
    stored_inputs = draw_stored_inputs(jax.random.fold_in(jax.random.fold_in(splits[7], part), 71), part)
    top_cotangent = bell_draw_with(part_splits[1], (SAMPLES, SEQ, D), 0.0625, 0.375, ((0, 8), (2, 2)), (0, 2, 8, 2.0))
    layer_weights = bell_draw(splits[2], (LAYERS, D, D), D ** -0.5, 0.125, ((1, 8), (2, 2)))
    block_layout = touch_ends((jax.random.randint(splits[3], (LAYERS, NB, NB), 0, 2) < 1).astype(jnp.int32), jax.random.fold_in(splits[3], 1), 0, 1)
    region_mask = draw_region_mask(jax.random.fold_in(splits[7], 71), part)
    partner_samples = draw_partner_samples(jax.random.fold_in(jax.random.fold_in(splits[7], part), 71), part)
    spins = touch_ends(jax.random.randint(part_splits[6], (SAMPLES, SEQ), 0, SPINS), jax.random.fold_in(part_splits[6], 1), 0, SPINS - 1).astype(jnp.int32)
    return {"stored_inputs": stored_inputs, "top_cotangent": top_cotangent, "layer_weights": layer_weights, "block_layout": block_layout, "region_mask": region_mask, "partner_samples": partner_samples, "spins": spins}


def rounded(value):
    return lax.optimization_barrier(value.astype(jnp.bfloat16)).astype(jnp.float32)


def layer_backward(grad_out, inputs, weight, allowed, attention_scale):
    head_count = D // HEAD
    inputs_h = inputs.astype(jnp.float32).reshape(SAMPLES, SEQ, head_count, HEAD)
    grad_attn = jnp.dot(grad_out.reshape(SAMPLES * SEQ, D), weight, preferred_element_type=jnp.float32)
    grad_attn = rounded(grad_attn).reshape(SAMPLES, SEQ, head_count, HEAD)
    scores = jnp.einsum('bqhd,bkhd->bhqk', inputs_h, inputs_h) * attention_scale
    scores = jnp.where(allowed, scores, -jnp.inf)
    top_score = jnp.max(scores, axis=-1, keepdims=True)
    expo_terms = jnp.exp(scores - top_score)
    probs = expo_terms / jnp.sum(expo_terms, axis=-1, keepdims=True)
    probs_low = rounded(probs)
    attended = rounded(jnp.einsum('bhqk,bkhd->bqhd', probs_low, inputs_h))
    grad_probs = jnp.einsum('bqhd,bkhd->bhqk', grad_attn, inputs_h)
    grad_scores = rounded(probs * (grad_probs - jnp.sum(grad_probs * probs, axis=-1, keepdims=True)))
    grad_in = grad_out.astype(jnp.float32).reshape(SAMPLES, SEQ, head_count, HEAD)
    grad_in = grad_in + jnp.einsum('bhqk,bqhd->bkhd', probs_low, grad_attn)
    grad_in = grad_in + attention_scale * (jnp.einsum('bhqk,bkhd->bqhd', grad_scores, inputs_h) + jnp.einsum('bhqk,bqhd->bkhd', grad_scores, inputs_h))
    return grad_in.reshape(SAMPLES, SEQ, D).astype(jnp.bfloat16), attended.reshape(SAMPLES, SEQ, D).astype(jnp.bfloat16)


def shard_term(total, pair):
    grad_rows, attended_rows = pair
    term = jnp.dot(grad_rows.T, attended_rows, preferred_element_type=jnp.float32)
    return total + rounded(term), None


def reference(stored_inputs, top_cotangent, layer_weights, block_layout, region_mask, partner_samples, spins):
    attention_scale = 4.0 / HEAD
    pos_block = jnp.arange(SEQ) // BLOCK
    grad_now = top_cotangent
    cotangents = [None] * LAYERS
    gradients = [None] * LAYERS
    for layer in reversed(range(LAYERS)):
        allowed = (block_layout[layer][pos_block[:, None], pos_block[None, :]] > 0) | (pos_block[:, None] == pos_block[None, :])
        grad_in, attended = layer_backward(grad_now, stored_inputs[layer], layer_weights[layer], allowed, attention_scale)
        grad_rows = grad_now.reshape(SHARDS, MB * SEQ, D)
        attended_rows = attended.reshape(SHARDS, MB * SEQ, D)
        total, unused = lax.scan(shard_term, jnp.zeros((D, D), jnp.float32), (grad_rows, attended_rows))
        gradients[layer] = total
        cotangents[layer] = grad_in
        grad_now = grad_in
    partner_ids = partner_samples.astype(jnp.int32)
    first = cotangents[0]
    site = jnp.where(region_mask[None, :, None] > 0, first[partner_ids], first)
    cotangents[0] = site
    onehot = (spins[:, :, None] == jnp.arange(SPINS, dtype=jnp.int32)[None, None, :]).astype(jnp.float32)
    embed_grad = jnp.einsum('btv,btd->vd', onehot, site.astype(jnp.float32))
    return jnp.stack(gradients), jnp.stack(cotangents), embed_grad
```

```python
import jax
import jax.numpy as jnp
from jax import lax
from jax.experimental import pallas as pl
from jax.experimental.pallas import tpu as pltpu
from jax.sharding import PartitionSpec as P

HEAD = 128
BLOCK = 64
SPINS = 2


def for_sending(value):

    def short(part):
        return part.astype(jnp.bfloat16) if part.dtype == jnp.float32 else part

    return jax.tree.map(short, value)


def passed_along(block, axis, distance):
    devices = range(lax.axis_size(axis))
    route = [(i - distance, i) for i in devices if i - distance in devices]
    return lax.ppermute(block, axis, route)


def softmax_parts(inputs_h, allowed, attention_scale):
    scores = (
        jnp.einsum("qhd,khd->hqk", inputs_h, inputs_h, preferred_element_type=jnp.float32)
        * attention_scale
    )
    scores = jnp.where(allowed[None], scores, -jnp.inf)
    top_score = jnp.max(scores, axis=-1, keepdims=True)
    expo_terms = jnp.exp(scores - top_score)
    probs = expo_terms / jnp.sum(expo_terms, axis=-1, keepdims=True)
    return (probs, probs.astype(jnp.bfloat16))


def local(
    stored_inputs, top_cotangent, layer_weights, block_layout, region_mask, partner_samples, spins
):
    section_index = lax.axis_index("section")
    section_count = lax.axis_size("section")
    micro_count = stored_inputs.shape[1]
    seq_len = stored_inputs.shape[2]
    half_width = stored_inputs.shape[3]
    head_count = half_width // HEAD
    attention_scale = 4.0 / HEAD
    weights = lax.all_gather(layer_weights[0], "samples", axis=0, tiled=True)
    pos_block = jnp.arange(seq_len) // BLOCK
    block_onehot = (pos_block[:, None] == jnp.arange(block_layout.shape[1])[None, :]).astype(
        jnp.float32
    )
    linked = jnp.dot(jnp.dot(block_onehot, block_layout[0].astype(jnp.float32)), block_onehot.T)
    allowed = (linked > 0.5) | (pos_block[:, None] == pos_block[None, :])
    every_layer_input = stored_inputs[0]
    inputs_h = every_layer_input[0].reshape(seq_len, head_count, HEAD)
    probs, probs_low = softmax_parts(inputs_h, allowed, attention_scale)
    attended = jnp.einsum(
        "hqk,khd->qhd", probs_low, inputs_h, preferred_element_type=jnp.float32
    ).astype(jnp.bfloat16)
    probs_list = [probs]
    low_list = [probs_low]
    attend_list = [attended.reshape(seq_len, half_width)]
    probs_all = jnp.stack(probs_list)
    low_all = jnp.stack(low_list)
    attend_store = jnp.stack(attend_list)

    def layer_back(grad_full, grad_own, inputs, probs, probs_low):
        grad_attn = jnp.dot(grad_full, weights, preferred_element_type=jnp.float32).astype(
            jnp.bfloat16
        )
        inputs_h = inputs.reshape(seq_len, head_count, HEAD)
        grad_h = grad_attn.reshape(seq_len, head_count, HEAD)
        grad_probs = jnp.einsum(
            "qhd,khd->hqk", grad_h, inputs_h, preferred_element_type=jnp.float32
        )
        grad_scores = (
            probs * (grad_probs - jnp.sum(grad_probs * probs, axis=-1, keepdims=True))
        ).astype(jnp.bfloat16)
        through = jnp.einsum("hqk,qhd->khd", probs_low, grad_h, preferred_element_type=jnp.float32)
        through = through + attention_scale * (
            jnp.einsum("hqk,khd->qhd", grad_scores, inputs_h, preferred_element_type=jnp.float32)
            + jnp.einsum("hqk,qhd->khd", grad_scores, inputs_h, preferred_element_type=jnp.float32)
        )
        grad_in = grad_own.astype(jnp.float32) + through.reshape(seq_len, half_width)
        return grad_in.astype(jnp.bfloat16)

    def resting(grad_full, grad_own, inputs, probs, probs_low):
        return jnp.zeros((seq_len, half_width), jnp.bfloat16)

    carried_state = jnp.zeros((seq_len, half_width), jnp.bfloat16)
    out_list = []
    grad_list = []
    total_steps = micro_count + section_count - 1
    for step_number in range(total_steps):
        micro_index = step_number - (section_count - 1 - section_index)
        active = (micro_index >= 0) & (micro_index < micro_count)
        slot_index = jnp.clip(micro_index, 0, micro_count - 1)
        from_top = lax.dynamic_index_in_dim(top_cotangent, slot_index, 0, keepdims=False)
        incoming = jnp.where(section_index == section_count - 1, from_top, carried_state)
        grad_full = lax.all_gather(incoming, "mp", axis=1, tiled=True)
        inputs_now = lax.dynamic_index_in_dim(every_layer_input, slot_index, 0, keepdims=False)
        probs_now = lax.dynamic_index_in_dim(probs_all, slot_index, 0, keepdims=False)
        low_now = lax.dynamic_index_in_dim(low_all, slot_index, 0, keepdims=False)
        grad_in = lax.cond(
            active, layer_back, resting, grad_full, incoming, inputs_now, probs_now, low_now
        )
        out_list.append(grad_in)
        grad_list.append(grad_full)
        if step_number < total_steps - 1:
            carried_state = jax.tree.map(
                lambda part, own: part.astype(own.dtype),
                passed_along(for_sending(grad_in), "section", -1),
                grad_in,
            )
    offset = section_count - 1 - section_index
    out_store = lax.dynamic_slice_in_dim(jnp.stack(out_list), offset, micro_count, 0)
    grad_store = lax.dynamic_slice_in_dim(jnp.stack(grad_list), offset, micro_count, 0)
    summed_weight = lax.psum_scatter(
        jnp.einsum(
            "mtf,mta->fa", grad_store, attend_store, preferred_element_type=jnp.float32
        ).astype(jnp.bfloat16),
        "samples",
        scatter_dimension=0,
        tiled=True,
    ).astype(jnp.float32)
    region_count = seq_len // 2
    rank_in_region = jnp.cumsum(region_mask) - 1
    select = (
        (rank_in_region[None, :] == jnp.arange(region_count)[:, None]) & (region_mask[None, :] > 0)
    ).astype(jnp.bfloat16)
    tiles = jnp.einsum("at,mtd->mad", select, out_store, preferred_element_type=jnp.float32).astype(
        jnp.bfloat16
    )
    shard_index = lax.axis_index("samples")
    my_partners = lax.dynamic_slice_in_dim(
        partner_samples, shard_index * micro_count, micro_count, 0
    )
    shard_count = lax.axis_size("samples")
    dest_shard = my_partners // micro_count
    dest_slot = my_partners % micro_count
    route = (
        (dest_shard[:, None, None] == jnp.arange(shard_count)[None, :, None])
        & (dest_slot[:, None, None] == jnp.arange(micro_count)[None, None, :])
    ).astype(jnp.bfloat16)
    outgoing = jnp.einsum("mku,mad->kuad", route, tiles, preferred_element_type=jnp.float32).astype(
        jnp.bfloat16
    )
    arrived = lax.all_to_all(outgoing, "samples", split_axis=0, concat_axis=0, tiled=True)
    ones_row = jnp.ones((shard_count,), jnp.bfloat16)
    received = jnp.einsum(
        "k,kuad->uad", ones_row, arrived, preferred_element_type=jnp.float32
    ).astype(jnp.bfloat16)
    placed = jnp.einsum("at,mad->mtd", select, received, preferred_element_type=jnp.float32)
    kept = jnp.where(region_mask[None, :, None] > 0, jnp.zeros_like(out_store), out_store)
    site_cot = (kept.astype(jnp.float32) + placed).astype(jnp.bfloat16)
    cotangents = jnp.where(section_index == 0, site_cot, out_store)
    onehot = (spins[:, :, None] == jnp.arange(SPINS)[None, None, :]).astype(jnp.bfloat16)
    embed_term = jnp.einsum("mtv,mtd->vd", onehot, site_cot, preferred_element_type=jnp.float32)
    embed_term = jnp.where(section_index == 0, embed_term, jnp.zeros_like(embed_term))
    embed_grad = lax.psum(embed_term, ("samples", "section"))
    return (summed_weight[None], cotangents[None], embed_grad)


NZ = 4
MESH = pl.DeviceIdType.MESH
F32 = jnp.float32
BF = jnp.bfloat16


def dot(a, b, ca=1, cb=0):
    return lax.dot_general(a, b, (((ca,), (cb,)), ((), ())), preferred_element_type=F32)


def kernel(
    x_ref, g_ref, w_ref, layout_ref, mask_ref, partner_ref, spin_ref,
    wg_ref, cot_ref, emb_ref,
    gq, w2, pf, pb, rl, rr, att, probs, ga, g0, tile, swz, xsend, xrecv,
    spall, embs, wsend, wrecv, wown,
    gq_s, gq_r, gf_s, gf_r, w_s, w_r, sp_s, sp_r, at_s, at_r, rs_s, rs_r,
    sw_s, sw_r, xs_s, xs_r, em_s, em_r, wr_s, wr_r,
):
    s = lax.axis_index("samples")
    m = lax.axis_index("mp")
    z = s // 2
    x = s % 2
    scale = 4.0 / HEAD
    tokens, width = x_ref.shape
    heads = width // HEAD
    rows = w_ref.shape[0]
    sibling = {"mp": 1 - m}
    beside = {"samples": 2 * z + 1 - x}

    def rdma(src, dst, ss, rs, dev):
        return pltpu.make_async_remote_copy(
            src_ref=src, dst_ref=dst, send_sem=ss, recv_sem=rs, device_id=dev, device_id_type=MESH
        )

    sends = []

    def send(cond, make):
        if cond is None:
            make().start()
        else:
            pl.when(cond)(lambda: make().start())
        sends.append((cond, make))

    def got(cond, dst, rs):
        def wait():
            rdma(dst, dst, rs, rs, sibling).wait_recv()

        if cond is None:
            wait()
        else:
            pl.when(cond)(wait)

    barrier = pltpu.get_barrier_semaphore()
    for k in range(1, 8):
        pl.semaphore_signal(
            barrier, inc=1, device_id={"samples": lax.rem(s + k, 8)}, device_id_type=MESH
        )
    pl.semaphore_signal(barrier, inc=1, device_id=sibling, device_id_type=MESH)
    pl.semaphore_wait(barrier, 8)

    half = width // 2
    for j in range(2):
        dz = 2 * m + j
        for_me = dz == z
        piece = g_ref.at[:, pl.ds(j * half, half)]
        send(
            jnp.logical_not(for_me),
            lambda piece=piece, dz=dz, j=j: rdma(
                piece, gq.at[z], gq_s.at[j], gq_r.at[z], {"samples": 2 * dz + x}
            ),
        )
        send(
            for_me,
            lambda piece=piece, j=j: rdma(piece, gq.at[z], gq_s.at[j], gf_r.at[z], sibling),
        )

        @pl.when(for_me)
        def _(j=j):
            gq[z] = g_ref[:, pl.ds(j * half, half)]

    send(None, lambda: rdma(w_ref, w2.at[x], w_s, w_r, beside))
    for k in range(1, 8):
        other = lax.rem(s + k, 8)
        send(
            None,
            lambda k=k, other=other: rdma(
                spin_ref, spall.at[s], sp_s.at[k], sp_r.at[s], {"samples": other}
            ),
        )
    w2[x] = w_ref[...]
    spall[s] = spin_ref[...]

    qb = lax.broadcasted_iota(jnp.int32, (tokens, tokens), 0) // BLOCK
    kb = lax.broadcasted_iota(jnp.int32, (tokens, tokens), 1) // BLOCK
    linked = jnp.where(qb < kb, layout_ref[0, 1], layout_ref[1, 0])
    allowed = (qb == kb) | (linked > 0)
    for h in range(heads):
        cols = pl.ds(h * HEAD, HEAD)
        xh = x_ref[:, cols]
        scores = jnp.where(allowed, dot(xh, xh, 1, 1) * scale, -jnp.inf)
        expo = jnp.exp(scores - jnp.max(scores, axis=-1, keepdims=True))
        p = expo / jnp.sum(expo, axis=-1, keepdims=True)
        probs[h] = p
        att[z, :, cols] = dot(p.astype(BF), xh).astype(BF)

    def att_hop(k):
        send(
            (z < NZ - 1) & (z - k >= 0),
            lambda: rdma(
                att.at[z - k], att.at[z - k], at_s.at[0, k], at_r.at[0, k], {"samples": s + 2}
            ),
        )
        send(
            (z > 0) & (z + k <= NZ - 1),
            lambda: rdma(
                att.at[z + k], att.at[z + k], at_s.at[1, k], at_r.at[1, k], {"samples": s - 2}
            ),
        )

    def att_wait(k):
        got(z - 1 - k >= 0, att.at[0], at_r.at[0, k])
        got(z + 1 + k <= NZ - 1, att.at[0], at_r.at[1, k])

    att_hop(0)

    first_core = m == z // 2
    for zz in range(NZ):
        near = first_core & (zz != z)
        got(near, gq.at[zz], gq_r.at[zz])
        send(near, lambda zz=zz: rdma(gq.at[zz], gq.at[zz], gf_s.at[zz], gf_r.at[zz], sibling))
    for zz in range(NZ):
        got(jnp.logical_not(first_core), gq.at[zz], gf_r.at[zz])
    got(None, w2.at[0], w_r)
    for d in (0, 3, 1, 2):
        part = dot(gq[d, :, :rows], w2[0]) + dot(gq[d, :, rows:], w2[1])
        pf[d] = part
        pb[d] = part.astype(BF)

    for d in range(NZ - 1):
        e = NZ - 1 - d
        relay = (z > d) & (z < NZ - 1)
        got(relay, rl.at[d], rs_r.at[0, d])

        @pl.when(relay)
        def _(d=d):
            pb[d] = (pf[d] + rl[d].astype(F32)).astype(BF)

        send(
            z > d,
            lambda d=d: rdma(pb.at[d], rl.at[d], rs_s.at[0, d], rs_r.at[0, d], {"samples": s - 2}),
        )
        relay = (z < e) & (z > 0)
        got(relay, rr.at[e], rs_r.at[1, e])

        @pl.when(relay)
        def _(e=e):
            pb[e] = (pf[e] + rr[e].astype(F32)).astype(BF)

        send(
            z < e,
            lambda e=e: rdma(pb.at[e], rr.at[e], rs_s.at[1, e], rs_r.at[1, e], {"samples": s + 2}),
        )

    att_wait(0)
    att_hop(1)

    for d in range(NZ - 1):
        got((z == d), rl.at[d], rs_r.at[0, d])
        got((z == d + 1), rr.at[d + 1], rs_r.at[1, d + 1])

    @pl.when(z == 0)
    def _():
        ga[...] = (pf[0] + rl[0].astype(F32)).astype(BF)

    @pl.when(z == NZ - 1)
    def _():
        ga[...] = (pf[NZ - 1] + rr[NZ - 1].astype(F32)).astype(BF)

    for d in range(1, NZ - 1):

        @pl.when(z == d)
        def _(d=d):
            ga[...] = (pf[d] + rl[d].astype(F32) + rr[d].astype(F32)).astype(BF)

    for h in range(heads):
        cols = pl.ds(h * HEAD, HEAD)
        xh = x_ref[:, cols]
        gh = ga[:, cols]
        p = probs[h]
        gp = dot(gh, xh, 1, 1)
        gs = (p * (gp - jnp.sum(gp * p, axis=-1, keepdims=True))).astype(BF)
        through = dot(p.astype(BF), gh, 0, 0) + scale * (dot(gs, xh) + dot(gs, xh, 0, 0))
        g0[:, cols] = (g_ref[:, cols].astype(F32) + through).astype(BF)

    mask = mask_ref[...]
    tri = (
        lax.broadcasted_iota(jnp.int32, (tokens, tokens), 0)
        <= lax.broadcasted_iota(jnp.int32, (tokens, tokens), 1)
    ).astype(F32).astype(BF)
    mask_rows = jnp.broadcast_to(mask, (8, tokens)).astype(F32)
    rank = dot(mask_rows.astype(BF), tri)[:1] - 1.0
    region = tokens // 2
    place = lax.broadcasted_iota(jnp.int32, (region, tokens), 0).astype(F32)
    select = jnp.where((rank == place) & (mask > 0), 1.0, 0.0).astype(BF)
    tile[...] = dot(select, g0[...]).astype(BF)
    for k in range(1, NZ):
        dz = lax.rem(z + k, NZ)
        send(
            None,
            lambda k=k, dz=dz: rdma(
                tile, swz.at[z], sw_s.at[k], sw_r.at[z], {"samples": 2 * dz + x}
            ),
        )
    swz[z] = tile[...]

    for k in range(1, 8):
        other = lax.rem(s + k, 8)
        got(None, spall.at[0], sp_r.at[other])
    mine = partner_ref[s]
    spins = jnp.where(mask > 0, spall[mine], spin_ref[...])
    onehot = jnp.where(
        spins == lax.broadcasted_iota(jnp.int32, (8, tokens), 0), 1.0, 0.0
    ).astype(BF)
    embs[s] = dot(onehot, g0[...])[:SPINS]
    for k in range(1, 8):
        other = lax.rem(s + k, 8)
        send(
            None,
            lambda k=k, other=other: rdma(
                embs.at[s], embs.at[s], em_s.at[k], em_r.at[s], {"samples": other}
            ),
        )

    att_wait(1)
    att_hop(2)
    att_wait(2)
    for c in range(4):
        cols = pl.ds(c * 256, 256)
        total = jnp.zeros((2 * rows, 256), F32)
        for zz in range(NZ):
            total += dot(gq[zz], att[zz, :, cols], 0, 0).astype(BF).astype(F32)

        @pl.when(x == 0)
        def _(cols=cols, total=total):
            wown[:, cols] = total[:rows]
            wsend[:, cols] = total[rows:].astype(BF)

        @pl.when(x == 1)
        def _(cols=cols, total=total):
            wown[:, cols] = total[rows:]
            wsend[:, cols] = total[:rows].astype(BF)

    send(None, lambda: rdma(wsend, wrecv, wr_s, wr_r, beside))

    for k in range(1, NZ):
        got(None, swz.at[0], sw_r.at[lax.rem(z + k, NZ)])
    theirs = partner_ref[2 * z + 1 - x]
    xsend[...] = swz[theirs // 2]
    send(None, lambda: rdma(xsend, xrecv, xs_s, xs_r, beside))
    same = jnp.where(mine % 2 == x, 1, 0)
    local_rows = swz[mine // 2]
    eye = lax.broadcasted_iota(jnp.int32, (tokens, tokens), 0) == lax.broadcasted_iota(
        jnp.int32, (tokens, tokens), 1
    )
    keep = jnp.where(eye & (mask == 0), 1.0, 0.0).astype(BF)
    kept = dot(keep, g0[...])
    for k in range(1, 8):
        got(None, embs.at[0], em_r.at[lax.rem(s + k, 8)])
    total = embs[0]
    for k in range(1, 8):
        total += embs[k]
    emb_ref[...] = total
    got(None, xrecv, xs_r)
    chosen = jnp.where(same > 0, local_rows, xrecv[...])
    cot_ref[...] = (kept + dot(select, chosen, 0, 0)).astype(BF)
    got(None, wrecv, wr_r)
    wg_ref[...] = wown[...] + wrecv[...].astype(F32)

    for cond, make in sends:
        if cond is None:
            make().wait_send()
        else:
            pl.when(cond)(lambda make=make: make().wait_send())


def one_layer(
    stored_inputs, top_cotangent, layer_weights, block_layout, region_mask, partner_samples, spins
):
    tokens, width = stored_inputs.shape[2:]
    rows = layer_weights.shape[1]
    vmem = pl.BlockSpec(memory_space=pltpu.VMEM)
    smem = pl.BlockSpec(memory_space=pltpu.SMEM)
    region = tokens // 2
    dma = pltpu.SemaphoreType.DMA
    shapes = [
        ((NZ, tokens, width // 2), BF),
        ((2, rows, width), BF),
        ((NZ, tokens, width), F32),
        ((NZ, tokens, width), BF),
        ((NZ, tokens, width), BF),
        ((NZ, tokens, width), BF),
        ((NZ, tokens, width), BF),
        ((width // HEAD, tokens, tokens), F32),
        ((tokens, width), BF),
        ((tokens, width), BF),
        ((region, width), BF),
        ((NZ, region, width), BF),
        ((region, width), BF),
        ((region, width), BF),
        ((8, 1, tokens), jnp.int32),
        ((8, SPINS, width), F32),
        ((rows, width), BF),
        ((rows, width), BF),
        ((rows, width), F32),
    ]
    sems = [
        dma((2,)), dma((NZ,)), dma((NZ,)), dma((NZ,)), dma, dma, dma((8,)), dma((8,)),
        dma((2, 3)), dma((2, 3)), dma((2, NZ)), dma((2, NZ)), dma((NZ,)), dma((NZ,)),
        dma, dma, dma((8,)), dma((8,)), dma, dma,
    ]
    wg, cot, emb = pl.pallas_call(
        kernel,
        out_shape=[
            jax.ShapeDtypeStruct((rows, width), F32),
            jax.ShapeDtypeStruct((tokens, width), BF),
            jax.ShapeDtypeStruct((SPINS, width), F32),
        ],
        in_specs=[vmem, vmem, vmem, smem, vmem, smem, vmem],
        out_specs=[vmem] * 3,
        scratch_shapes=[pltpu.VMEM(a, b) for a, b in shapes] + sems,
        compiler_params=pltpu.CompilerParams(
            collective_id=0, has_side_effects=True, vmem_limit_bytes=48 * 1024 * 1024
        ),
    )(
        stored_inputs[0, 0], top_cotangent[0], layer_weights[0], block_layout[0],
        region_mask[None], partner_samples, spins,
    )
    return wg[None], cot[None, None], emb


def solution(mesh):
    in_specs = (
        P("section", ("groups", "samples"), None, "mp"),
        P(("groups", "samples"), None, "mp"),
        P("section", "samples", "mp"),
        P("section", None, None),
        P(),
        P("groups"),
        P(("groups", "samples"), None),
    )
    out_specs = (
        P(("groups", "section"), "samples", "mp"),
        P("section", ("groups", "samples"), None, "mp"),
        P("groups", "mp"),
    )
    small = mesh.shape["samples"] == 8 and mesh.shape["section"] == 1 and mesh.shape["mp"] == 2
    body = one_layer if small else local
    return jax.shard_map(body, mesh=mesh, in_specs=in_specs, out_specs=out_specs, check_vma=False)
```

```python
import jax
import jax.numpy as jnp
from jax import lax
from jax.experimental import pallas as pl
from jax.experimental.pallas import tpu as pltpu
from jax.sharding import PartitionSpec as P

HEAD = 128
BLOCK = 64
SPINS = 2


def for_sending(value):

    def short(part):
        return part.astype(jnp.bfloat16) if part.dtype == jnp.float32 else part

    return jax.tree.map(short, value)


def passed_along(block, axis, distance):
    devices = range(lax.axis_size(axis))
    route = [(i - distance, i) for i in devices if i - distance in devices]
    return lax.ppermute(block, axis, route)


def softmax_parts(inputs_h, allowed, attention_scale):
    scores = (
        jnp.einsum("qhd,khd->hqk", inputs_h, inputs_h, preferred_element_type=jnp.float32)
        * attention_scale
    )
    scores = jnp.where(allowed[None], scores, -jnp.inf)
    top_score = jnp.max(scores, axis=-1, keepdims=True)
    expo_terms = jnp.exp(scores - top_score)
    probs = expo_terms / jnp.sum(expo_terms, axis=-1, keepdims=True)
    return (probs, probs.astype(jnp.bfloat16))


def local(
    stored_inputs, top_cotangent, layer_weights, block_layout, region_mask, partner_samples, spins
):
    section_index = lax.axis_index("section")
    section_count = lax.axis_size("section")
    micro_count = stored_inputs.shape[1]
    seq_len = stored_inputs.shape[2]
    half_width = stored_inputs.shape[3]
    head_count = half_width // HEAD
    attention_scale = 4.0 / HEAD
    weights = lax.all_gather(layer_weights[0], "samples", axis=0, tiled=True)
    pos_block = jnp.arange(seq_len) // BLOCK
    block_onehot = (pos_block[:, None] == jnp.arange(block_layout.shape[1])[None, :]).astype(
        jnp.float32
    )
    linked = jnp.dot(jnp.dot(block_onehot, block_layout[0].astype(jnp.float32)), block_onehot.T)
    allowed = (linked > 0.5) | (pos_block[:, None] == pos_block[None, :])
    every_layer_input = stored_inputs[0]
    inputs_h = every_layer_input[0].reshape(seq_len, head_count, HEAD)
    probs, probs_low = softmax_parts(inputs_h, allowed, attention_scale)
    attended = jnp.einsum(
        "hqk,khd->qhd", probs_low, inputs_h, preferred_element_type=jnp.float32
    ).astype(jnp.bfloat16)
    probs_list = [probs]
    low_list = [probs_low]
    attend_list = [attended.reshape(seq_len, half_width)]
    probs_all = jnp.stack(probs_list)
    low_all = jnp.stack(low_list)
    attend_store = jnp.stack(attend_list)

    def layer_back(grad_full, grad_own, inputs, probs, probs_low):
        grad_attn = jnp.dot(grad_full, weights, preferred_element_type=jnp.float32).astype(
            jnp.bfloat16
        )
        inputs_h = inputs.reshape(seq_len, head_count, HEAD)
        grad_h = grad_attn.reshape(seq_len, head_count, HEAD)
        grad_probs = jnp.einsum(
            "qhd,khd->hqk", grad_h, inputs_h, preferred_element_type=jnp.float32
        )
        grad_scores = (
            probs * (grad_probs - jnp.sum(grad_probs * probs, axis=-1, keepdims=True))
        ).astype(jnp.bfloat16)
        through = jnp.einsum("hqk,qhd->khd", probs_low, grad_h, preferred_element_type=jnp.float32)
        through = through + attention_scale * (
            jnp.einsum("hqk,khd->qhd", grad_scores, inputs_h, preferred_element_type=jnp.float32)
            + jnp.einsum("hqk,qhd->khd", grad_scores, inputs_h, preferred_element_type=jnp.float32)
        )
        grad_in = grad_own.astype(jnp.float32) + through.reshape(seq_len, half_width)
        return grad_in.astype(jnp.bfloat16)

    def resting(grad_full, grad_own, inputs, probs, probs_low):
        return jnp.zeros((seq_len, half_width), jnp.bfloat16)

    carried_state = jnp.zeros((seq_len, half_width), jnp.bfloat16)
    out_list = []
    grad_list = []
    total_steps = micro_count + section_count - 1
    for step_number in range(total_steps):
        micro_index = step_number - (section_count - 1 - section_index)
        active = (micro_index >= 0) & (micro_index < micro_count)
        slot_index = jnp.clip(micro_index, 0, micro_count - 1)
        from_top = lax.dynamic_index_in_dim(top_cotangent, slot_index, 0, keepdims=False)
        incoming = jnp.where(section_index == section_count - 1, from_top, carried_state)
        grad_full = lax.all_gather(incoming, "mp", axis=1, tiled=True)
        inputs_now = lax.dynamic_index_in_dim(every_layer_input, slot_index, 0, keepdims=False)
        probs_now = lax.dynamic_index_in_dim(probs_all, slot_index, 0, keepdims=False)
        low_now = lax.dynamic_index_in_dim(low_all, slot_index, 0, keepdims=False)
        grad_in = lax.cond(
            active, layer_back, resting, grad_full, incoming, inputs_now, probs_now, low_now
        )
        out_list.append(grad_in)
        grad_list.append(grad_full)
        if step_number < total_steps - 1:
            carried_state = jax.tree.map(
                lambda part, own: part.astype(own.dtype),
                passed_along(for_sending(grad_in), "section", -1),
                grad_in,
            )
    offset = section_count - 1 - section_index
    out_store = lax.dynamic_slice_in_dim(jnp.stack(out_list), offset, micro_count, 0)
    grad_store = lax.dynamic_slice_in_dim(jnp.stack(grad_list), offset, micro_count, 0)
    summed_weight = lax.psum_scatter(
        jnp.einsum(
            "mtf,mta->fa", grad_store, attend_store, preferred_element_type=jnp.float32
        ).astype(jnp.bfloat16),
        "samples",
        scatter_dimension=0,
        tiled=True,
    ).astype(jnp.float32)
    region_count = seq_len // 2
    rank_in_region = jnp.cumsum(region_mask) - 1
    select = (
        (rank_in_region[None, :] == jnp.arange(region_count)[:, None]) & (region_mask[None, :] > 0)
    ).astype(jnp.bfloat16)
    tiles = jnp.einsum("at,mtd->mad", select, out_store, preferred_element_type=jnp.float32).astype(
        jnp.bfloat16
    )
    shard_index = lax.axis_index("samples")
    my_partners = lax.dynamic_slice_in_dim(
        partner_samples, shard_index * micro_count, micro_count, 0
    )
    shard_count = lax.axis_size("samples")
    dest_shard = my_partners // micro_count
    dest_slot = my_partners % micro_count
    route = (
        (dest_shard[:, None, None] == jnp.arange(shard_count)[None, :, None])
        & (dest_slot[:, None, None] == jnp.arange(micro_count)[None, None, :])
    ).astype(jnp.bfloat16)
    outgoing = jnp.einsum("mku,mad->kuad", route, tiles, preferred_element_type=jnp.float32).astype(
        jnp.bfloat16
    )
    arrived = lax.all_to_all(outgoing, "samples", split_axis=0, concat_axis=0, tiled=True)
    ones_row = jnp.ones((shard_count,), jnp.bfloat16)
    received = jnp.einsum(
        "k,kuad->uad", ones_row, arrived, preferred_element_type=jnp.float32
    ).astype(jnp.bfloat16)
    placed = jnp.einsum("at,mad->mtd", select, received, preferred_element_type=jnp.float32)
    kept = jnp.where(region_mask[None, :, None] > 0, jnp.zeros_like(out_store), out_store)
    site_cot = (kept.astype(jnp.float32) + placed).astype(jnp.bfloat16)
    cotangents = jnp.where(section_index == 0, site_cot, out_store)
    onehot = (spins[:, :, None] == jnp.arange(SPINS)[None, None, :]).astype(jnp.bfloat16)
    embed_term = jnp.einsum("mtv,mtd->vd", onehot, site_cot, preferred_element_type=jnp.float32)
    embed_term = jnp.where(section_index == 0, embed_term, jnp.zeros_like(embed_term))
    embed_grad = lax.psum(embed_term, ("samples", "section"))
    return (summed_weight[None], cotangents[None], embed_grad)


NZ = 4
MESH = pl.DeviceIdType.MESH
F32 = jnp.float32
BF = jnp.bfloat16


def dot(a, b, ca=1, cb=0):
    return lax.dot_general(a, b, (((ca,), (cb,)), ((), ())), preferred_element_type=F32)


def kernel(
    x_hbm, g_hbm, w_hbm, layout_ref, mask_ref, partner_ref, spin_ref,
    wg_ref, cot_ref, emb_ref,
    x_ref, g_ref, gq, w2, pf, pb, rl, rr, att, probs, ga, g0, tile, swz, xsend, xrecv,
    spall, embs, wsend, wrecv, wown,
    in_s, gq_s, gq_r, gf_s, gf_r, w_s, w_r, sp_s, sp_r, at_s, at_r, rs_s, rs_r,
    sw_s, sw_r, xs_s, xs_r, em_s, em_r, wr_s, wr_r,
):
    s = lax.axis_index("samples")
    m = lax.axis_index("mp")
    z = s // 2
    x = s % 2
    scale = 4.0 / HEAD
    tokens, width = x_ref.shape
    heads = width // HEAD
    rows = w_hbm.shape[0]
    half = width // 2
    sibling = {"mp": 1 - m}
    beside = {"samples": 2 * z + 1 - x}

    def rdma(src, dst, ss, rs, dev):
        return pltpu.make_async_remote_copy(
            src_ref=src, dst_ref=dst, send_sem=ss, recv_sem=rs, device_id=dev, device_id_type=MESH
        )

    sends = []

    def send(cond, make):
        if cond is None:
            make().start()
        else:
            pl.when(cond)(lambda: make().start())
        sends.append((cond, make))

    def got(cond, dst, rs):
        def wait():
            rdma(dst, dst, rs, rs, sibling).wait_recv()

        if cond is None:
            wait()
        else:
            pl.when(cond)(wait)

    loads = [
        pltpu.make_async_copy(g_hbm, g_ref, in_s.at[0]),
        pltpu.make_async_copy(w_hbm, w2.at[x], in_s.at[1]),
        pltpu.make_async_copy(x_hbm, x_ref, in_s.at[2]),
    ]
    for load in loads:
        load.start()
    barrier = pltpu.get_barrier_semaphore()
    for k in range(1, 8):
        pl.semaphore_signal(
            barrier, inc=1, device_id={"samples": lax.rem(s + k, 8)}, device_id_type=MESH
        )
    pl.semaphore_signal(barrier, inc=1, device_id=sibling, device_id_type=MESH)
    pl.semaphore_wait(barrier, 8)

    loads[0].wait()
    for j in range(2):
        dz = 2 * m + j
        for_me = dz == z
        piece = g_ref.at[:, pl.ds(j * half, half)]
        send(
            jnp.logical_not(for_me),
            lambda piece=piece, dz=dz, j=j: rdma(
                piece, gq.at[z], gq_s.at[j], gq_r.at[z], {"samples": 2 * dz + x}
            ),
        )
        send(
            for_me,
            lambda piece=piece, j=j: rdma(piece, gq.at[z], gq_s.at[j], gf_r.at[z], sibling),
        )

        @pl.when(for_me)
        def _(j=j):
            gq[z] = g_ref[:, pl.ds(j * half, half)]

    loads[1].wait()
    for c in range(2):
        block = w2.at[x, :, pl.ds(c * half, half)]
        send(None, lambda block=block, c=c: rdma(block, block, w_s.at[c], w_r.at[c], beside))
    for k in range(1, 8):
        other = lax.rem(s + k, 8)
        send(
            None,
            lambda k=k, other=other: rdma(
                spin_ref, spall.at[s], sp_s.at[k], sp_r.at[s], {"samples": other}
            ),
        )
    spall[s] = spin_ref[...]

    loads[2].wait()
    qb = lax.broadcasted_iota(jnp.int32, (tokens, tokens), 0) // BLOCK
    kb = lax.broadcasted_iota(jnp.int32, (tokens, tokens), 1) // BLOCK
    linked = jnp.where(qb < kb, layout_ref[0, 1], layout_ref[1, 0])
    allowed = (qb == kb) | (linked > 0)
    for h in range(heads):
        cols = pl.ds(h * HEAD, HEAD)
        xh = x_ref[:, cols]
        scores = jnp.where(allowed, dot(xh, xh, 1, 1) * scale, -jnp.inf)
        expo = jnp.exp(scores - jnp.max(scores, axis=-1, keepdims=True))
        p = expo / jnp.sum(expo, axis=-1, keepdims=True)
        probs[h] = p
        att[z, :, cols] = dot(p.astype(BF), xh).astype(BF)

    def att_hop(k):
        send(
            (z < NZ - 1) & (z - k >= 0),
            lambda: rdma(
                att.at[z - k], att.at[z - k], at_s.at[0, k], at_r.at[0, k], {"samples": s + 2}
            ),
        )
        send(
            (z > 0) & (z + k <= NZ - 1),
            lambda: rdma(
                att.at[z + k], att.at[z + k], at_s.at[1, k], at_r.at[1, k], {"samples": s - 2}
            ),
        )

    def att_wait(k):
        got(z - 1 - k >= 0, att.at[0], at_r.at[0, k])
        got(z + 1 + k <= NZ - 1, att.at[0], at_r.at[1, k])

    att_hop(0)

    first_core = m == z // 2
    for zz in range(NZ):
        near = first_core & (zz != z)
        got(near, gq.at[zz], gq_r.at[zz])
        send(near, lambda zz=zz: rdma(gq.at[zz], gq.at[zz], gf_s.at[zz], gf_r.at[zz], sibling))
    for zz in range(NZ):
        got(jnp.logical_not(first_core), gq.at[zz], gf_r.at[zz])

    def partials(c):
        got(None, w2.at[0, :, pl.ds(c * half, half)], w_r.at[c])
        cols = pl.ds(c * half, half)
        for d in range(NZ):
            part = dot(gq[d, :, :rows], w2[0, :, cols]) + dot(gq[d, :, rows:], w2[1, :, cols])
            pf[c, d] = part
            pb[c, d] = part.astype(BF)
        for d in range(NZ - 1):
            e = NZ - 1 - d
            send(
                z == NZ - 1,
                lambda d=d: rdma(
                    pb.at[c, d], rl.at[c, d], rs_s.at[0, c, d], rs_r.at[0, c, d], {"samples": s - 2}
                ),
            )
            send(
                z == 0,
                lambda e=e: rdma(
                    pb.at[c, e], rr.at[c, e], rs_s.at[1, c, e], rs_r.at[1, c, e], {"samples": s + 2}
                ),
            )

    def relay_left(c, at, d):
        here = z == at
        got(here, rl.at[c, d], rs_r.at[0, c, d])

        @pl.when(here)
        def _():
            pb[c, d] = (pf[c, d] + rl[c, d].astype(F32)).astype(BF)

        send(
            here,
            lambda: rdma(
                pb.at[c, d], rl.at[c, d], rs_s.at[0, c, d], rs_r.at[0, c, d], {"samples": s - 2}
            ),
        )

    def relay_right(c, at, e):
        here = z == at
        got(here, rr.at[c, e], rs_r.at[1, c, e])

        @pl.when(here)
        def _():
            pb[c, e] = (pf[c, e] + rr[c, e].astype(F32)).astype(BF)

        send(
            here,
            lambda: rdma(
                pb.at[c, e], rr.at[c, e], rs_s.at[1, c, e], rs_r.at[1, c, e], {"samples": s + 2}
            ),
        )

    def relays_near(c):
        relay_left(c, 2, 0)
        relay_right(c, 1, 3)
        relay_left(c, 2, 1)
        relay_right(c, 1, 2)

    def relays_far(c):
        relay_left(c, 1, 0)
        relay_right(c, 2, 3)

    partials(0)
    att_wait(0)
    att_hop(1)
    partials(1)
    relays_near(0)
    att_wait(1)
    att_hop(2)
    relays_far(0)
    relays_near(1)

    att_wait(2)
    for c in range(4):
        cols = pl.ds(c * 256, 256)
        total = jnp.zeros((2 * rows, 256), F32)
        for zz in range(NZ):
            total += dot(gq[zz], att[zz, :, cols], 0, 0).astype(BF).astype(F32)

        @pl.when(x == 0)
        def _(cols=cols, total=total):
            wown[:, cols] = total[:rows]
            wsend[:, cols] = total[rows:].astype(BF)

        @pl.when(x == 1)
        def _(cols=cols, total=total):
            wown[:, cols] = total[rows:]
            wsend[:, cols] = total[:rows].astype(BF)

    send(None, lambda: rdma(wsend, wrecv, wr_s, wr_r, beside))


    relays_far(1)

    mask = mask_ref[...]
    tri = (
        lax.broadcasted_iota(jnp.int32, (tokens, tokens), 0)
        <= lax.broadcasted_iota(jnp.int32, (tokens, tokens), 1)
    ).astype(F32).astype(BF)
    mask_rows = jnp.broadcast_to(mask, (8, tokens)).astype(F32)
    rank = dot(mask_rows.astype(BF), tri)[:1] - 1.0
    region = tokens // 2
    place = lax.broadcasted_iota(jnp.int32, (region, tokens), 0).astype(F32)
    select = jnp.where((rank == place) & (mask > 0), 1.0, 0.0).astype(BF)

    def backward(c):
        for d in range(NZ - 1):
            got((z == d), rl.at[c, d], rs_r.at[0, c, d])
            got((z == d + 1), rr.at[c, d + 1], rs_r.at[1, c, d + 1])
        for d in range(NZ):

            @pl.when(z == d)
            def _(d=d):
                total = pf[c, d]
                if d < NZ - 1:
                    total += rl[c, d].astype(F32)
                if d > 0:
                    total += rr[c, d].astype(F32)
                ga[...] = total.astype(BF)

        for h in range(heads // 2):
            cols = pl.ds(c * half + h * HEAD, HEAD)
            xh = x_ref[:, cols]
            gh = ga[:, h * HEAD : (h + 1) * HEAD]
            p = probs[c * (heads // 2) + h]
            gp = dot(gh, xh, 1, 1)
            gs = (p * (gp - jnp.sum(gp * p, axis=-1, keepdims=True))).astype(BF)
            through = dot(p.astype(BF), gh, 0, 0) + scale * (dot(gs, xh) + dot(gs, xh, 0, 0))
            g0[:, cols] = (g_ref[:, cols].astype(F32) + through).astype(BF)
        tile[c] = dot(select, g0[:, pl.ds(c * half, half)]).astype(BF)
        for k in range(1, NZ):
            dz = lax.rem(z + k, NZ)
            send(
                None,
                lambda k=k, dz=dz: rdma(
                    tile.at[c], swz.at[c, z], sw_s.at[c, k], sw_r.at[c, z], {"samples": 2 * dz + x}
                ),
            )
        swz[c, z] = tile[c]

    backward(0)
    backward(1)

    for k in range(1, 8):
        other = lax.rem(s + k, 8)
        got(None, spall.at[0], sp_r.at[other])
    mine = partner_ref[s]
    spins = jnp.where(mask > 0, spall[mine], spin_ref[...])
    onehot = jnp.where(
        spins == lax.broadcasted_iota(jnp.int32, (8, tokens), 0), 1.0, 0.0
    ).astype(BF)
    embs[s] = dot(onehot, g0[...])[:SPINS]
    for k in range(1, 8):
        other = lax.rem(s + k, 8)
        send(
            None,
            lambda k=k, other=other: rdma(
                embs.at[s], embs.at[s], em_s.at[k], em_r.at[s], {"samples": other}
            ),
        )

    def rows_from(c, which):
        rows_now = swz[c, 0]
        for zz in range(1, NZ):
            rows_now = jnp.where(which == zz, swz[c, zz], rows_now)
        return rows_now

    theirs = partner_ref[2 * z + 1 - x]
    for c in range(2):
        for k in range(1, NZ):
            got(None, swz.at[c, 0], sw_r.at[c, lax.rem(z + k, NZ)])
        xsend[c] = rows_from(c, theirs // 2)
        send(
            None, lambda c=c: rdma(xsend.at[c], xrecv.at[c], xs_s.at[c], xs_r.at[c], beside)
        )
    same = jnp.where(mine % 2 == x, 1, 0)
    eye = lax.broadcasted_iota(jnp.int32, (tokens, tokens), 0) == lax.broadcasted_iota(
        jnp.int32, (tokens, tokens), 1
    )
    keep = jnp.where(eye & (mask == 0), 1.0, 0.0).astype(BF)
    kept = dot(keep, g0[...])
    for k in range(1, 8):
        got(None, embs.at[0], em_r.at[lax.rem(s + k, 8)])
    total = embs[0]
    for k in range(1, 8):
        total += embs[k]
    emb_ref[...] = total
    got(None, wrecv, wr_r)
    wg_ref[...] = wown[...] + wrecv[...].astype(F32)
    for c in range(2):
        cols = slice(c * half, (c + 1) * half)
        got(None, xrecv.at[c], xs_r.at[c])
        chosen = jnp.where(same > 0, rows_from(c, mine // 2), xrecv[c])
        cot_ref[:, cols] = (kept[:, cols] + dot(select, chosen, 0, 0)).astype(BF)

    for cond, make in sends:
        if cond is None:
            make().wait_send()
        else:
            pl.when(cond)(lambda make=make: make().wait_send())


def one_layer(
    stored_inputs, top_cotangent, layer_weights, block_layout, region_mask, partner_samples, spins
):
    tokens, width = stored_inputs.shape[2:]
    rows = layer_weights.shape[1]
    hbm = pl.BlockSpec(memory_space=pltpu.HBM)
    vmem = pl.BlockSpec(memory_space=pltpu.VMEM)
    smem = pl.BlockSpec(memory_space=pltpu.SMEM)
    region = tokens // 2
    dma = pltpu.SemaphoreType.DMA
    half = width // 2
    shapes = [
        ((tokens, width), BF),
        ((tokens, width), BF),
        ((NZ, tokens, half), BF),
        ((2, rows, width), BF),
        ((2, NZ, tokens, half), F32),
        ((2, NZ, tokens, half), BF),
        ((2, NZ, tokens, half), BF),
        ((2, NZ, tokens, half), BF),
        ((NZ, tokens, width), BF),
        ((width // HEAD, tokens, tokens), F32),
        ((tokens, half), BF),
        ((tokens, width), BF),
        ((2, region, half), BF),
        ((2, NZ, region, half), BF),
        ((2, region, half), BF),
        ((2, region, half), BF),
        ((8, 1, tokens), jnp.int32),
        ((8, SPINS, width), F32),
        ((rows, width), BF),
        ((rows, width), BF),
        ((rows, width), F32),
    ]
    sems = [
        dma((3,)), dma((2,)), dma((NZ,)), dma((NZ,)), dma((NZ,)), dma((2,)), dma((2,)),
        dma((8,)), dma((8,)), dma((2, 3)), dma((2, 3)), dma((2, 2, NZ)), dma((2, 2, NZ)),
        dma((2, NZ)), dma((2, NZ)), dma((2,)), dma((2,)), dma((8,)), dma((8,)), dma, dma,
    ]
    wg, cot, emb = pl.pallas_call(
        kernel,
        out_shape=[
            jax.ShapeDtypeStruct((rows, width), F32),
            jax.ShapeDtypeStruct((tokens, width), BF),
            jax.ShapeDtypeStruct((SPINS, width), F32),
        ],
        in_specs=[hbm, hbm, hbm, smem, vmem, smem, vmem],
        out_specs=[vmem] * 3,
        scratch_shapes=[pltpu.VMEM(a, b) for a, b in shapes] + sems,
        compiler_params=pltpu.CompilerParams(
            collective_id=0, has_side_effects=True, vmem_limit_bytes=48 * 1024 * 1024
        ),
    )(
        stored_inputs[0, 0], top_cotangent[0], layer_weights[0], block_layout[0],
        region_mask[None], partner_samples, spins,
    )
    return wg[None], cot[None, None], emb


def solution(mesh):
    in_specs = (
        P("section", ("groups", "samples"), None, "mp"),
        P(("groups", "samples"), None, "mp"),
        P("section", "samples", "mp"),
        P("section", None, None),
        P(),
        P("groups"),
        P(("groups", "samples"), None),
    )
    out_specs = (
        P(("groups", "section"), "samples", "mp"),
        P("section", ("groups", "samples"), None, "mp"),
        P("groups", "mp"),
    )
    small = mesh.shape["samples"] == 8 and mesh.shape["section"] == 1 and mesh.shape["mp"] == 2
    body = one_layer if small else local
    return jax.shard_map(body, mesh=mesh, in_specs=in_specs, out_specs=out_specs, check_vma=False)
```

```python
import jax
import jax.numpy as jnp
from jax import lax
from jax.experimental import pallas as pl
from jax.experimental.pallas import tpu as pltpu
from jax.sharding import PartitionSpec as P

HEAD = 128
BLOCK = 64
SPINS = 2


def for_sending(value):

    def short(part):
        return part.astype(jnp.bfloat16) if part.dtype == jnp.float32 else part

    return jax.tree.map(short, value)


def passed_along(block, axis, distance):
    devices = range(lax.axis_size(axis))
    route = [(i - distance, i) for i in devices if i - distance in devices]
    return lax.ppermute(block, axis, route)


def softmax_parts(inputs_h, allowed, attention_scale):
    scores = (
        jnp.einsum("qhd,khd->hqk", inputs_h, inputs_h, preferred_element_type=jnp.float32)
        * attention_scale
    )
    scores = jnp.where(allowed[None], scores, -jnp.inf)
    top_score = jnp.max(scores, axis=-1, keepdims=True)
    expo_terms = jnp.exp(scores - top_score)
    probs = expo_terms / jnp.sum(expo_terms, axis=-1, keepdims=True)
    return (probs, probs.astype(jnp.bfloat16))


def local(
    stored_inputs, top_cotangent, layer_weights, block_layout, region_mask, partner_samples, spins
):
    section_index = lax.axis_index("section")
    section_count = lax.axis_size("section")
    micro_count = stored_inputs.shape[1]
    seq_len = stored_inputs.shape[2]
    half_width = stored_inputs.shape[3]
    head_count = half_width // HEAD
    attention_scale = 4.0 / HEAD
    weights = lax.all_gather(layer_weights[0], "samples", axis=0, tiled=True)
    pos_block = jnp.arange(seq_len) // BLOCK
    block_onehot = (pos_block[:, None] == jnp.arange(block_layout.shape[1])[None, :]).astype(
        jnp.float32
    )
    linked = jnp.dot(jnp.dot(block_onehot, block_layout[0].astype(jnp.float32)), block_onehot.T)
    allowed = (linked > 0.5) | (pos_block[:, None] == pos_block[None, :])
    every_layer_input = stored_inputs[0]
    inputs_h = every_layer_input[0].reshape(seq_len, head_count, HEAD)
    probs, probs_low = softmax_parts(inputs_h, allowed, attention_scale)
    attended = jnp.einsum(
        "hqk,khd->qhd", probs_low, inputs_h, preferred_element_type=jnp.float32
    ).astype(jnp.bfloat16)
    probs_list = [probs]
    low_list = [probs_low]
    attend_list = [attended.reshape(seq_len, half_width)]
    probs_all = jnp.stack(probs_list)
    low_all = jnp.stack(low_list)
    attend_store = jnp.stack(attend_list)

    def layer_back(grad_full, grad_own, inputs, probs, probs_low):
        grad_attn = jnp.dot(grad_full, weights, preferred_element_type=jnp.float32).astype(
            jnp.bfloat16
        )
        inputs_h = inputs.reshape(seq_len, head_count, HEAD)
        grad_h = grad_attn.reshape(seq_len, head_count, HEAD)
        grad_probs = jnp.einsum(
            "qhd,khd->hqk", grad_h, inputs_h, preferred_element_type=jnp.float32
        )
        grad_scores = (
            probs * (grad_probs - jnp.sum(grad_probs * probs, axis=-1, keepdims=True))
        ).astype(jnp.bfloat16)
        through = jnp.einsum("hqk,qhd->khd", probs_low, grad_h, preferred_element_type=jnp.float32)
        through = through + attention_scale * (
            jnp.einsum("hqk,khd->qhd", grad_scores, inputs_h, preferred_element_type=jnp.float32)
            + jnp.einsum("hqk,qhd->khd", grad_scores, inputs_h, preferred_element_type=jnp.float32)
        )
        grad_in = grad_own.astype(jnp.float32) + through.reshape(seq_len, half_width)
        return grad_in.astype(jnp.bfloat16)

    def resting(grad_full, grad_own, inputs, probs, probs_low):
        return jnp.zeros((seq_len, half_width), jnp.bfloat16)

    carried_state = jnp.zeros((seq_len, half_width), jnp.bfloat16)
    out_list = []
    grad_list = []
    total_steps = micro_count + section_count - 1
    for step_number in range(total_steps):
        micro_index = step_number - (section_count - 1 - section_index)
        active = (micro_index >= 0) & (micro_index < micro_count)
        slot_index = jnp.clip(micro_index, 0, micro_count - 1)
        from_top = lax.dynamic_index_in_dim(top_cotangent, slot_index, 0, keepdims=False)
        incoming = jnp.where(section_index == section_count - 1, from_top, carried_state)
        grad_full = lax.all_gather(incoming, "mp", axis=1, tiled=True)
        inputs_now = lax.dynamic_index_in_dim(every_layer_input, slot_index, 0, keepdims=False)
        probs_now = lax.dynamic_index_in_dim(probs_all, slot_index, 0, keepdims=False)
        low_now = lax.dynamic_index_in_dim(low_all, slot_index, 0, keepdims=False)
        grad_in = lax.cond(
            active, layer_back, resting, grad_full, incoming, inputs_now, probs_now, low_now
        )
        out_list.append(grad_in)
        grad_list.append(grad_full)
        if step_number < total_steps - 1:
            carried_state = jax.tree.map(
                lambda part, own: part.astype(own.dtype),
                passed_along(for_sending(grad_in), "section", -1),
                grad_in,
            )
    offset = section_count - 1 - section_index
    out_store = lax.dynamic_slice_in_dim(jnp.stack(out_list), offset, micro_count, 0)
    grad_store = lax.dynamic_slice_in_dim(jnp.stack(grad_list), offset, micro_count, 0)
    summed_weight = lax.psum_scatter(
        jnp.einsum(
            "mtf,mta->fa", grad_store, attend_store, preferred_element_type=jnp.float32
        ).astype(jnp.bfloat16),
        "samples",
        scatter_dimension=0,
        tiled=True,
    ).astype(jnp.float32)
    region_count = seq_len // 2
    rank_in_region = jnp.cumsum(region_mask) - 1
    select = (
        (rank_in_region[None, :] == jnp.arange(region_count)[:, None]) & (region_mask[None, :] > 0)
    ).astype(jnp.bfloat16)
    tiles = jnp.einsum("at,mtd->mad", select, out_store, preferred_element_type=jnp.float32).astype(
        jnp.bfloat16
    )
    shard_index = lax.axis_index("samples")
    my_partners = lax.dynamic_slice_in_dim(
        partner_samples, shard_index * micro_count, micro_count, 0
    )
    shard_count = lax.axis_size("samples")
    dest_shard = my_partners // micro_count
    dest_slot = my_partners % micro_count
    route = (
        (dest_shard[:, None, None] == jnp.arange(shard_count)[None, :, None])
        & (dest_slot[:, None, None] == jnp.arange(micro_count)[None, None, :])
    ).astype(jnp.bfloat16)
    outgoing = jnp.einsum("mku,mad->kuad", route, tiles, preferred_element_type=jnp.float32).astype(
        jnp.bfloat16
    )
    arrived = lax.all_to_all(outgoing, "samples", split_axis=0, concat_axis=0, tiled=True)
    ones_row = jnp.ones((shard_count,), jnp.bfloat16)
    received = jnp.einsum(
        "k,kuad->uad", ones_row, arrived, preferred_element_type=jnp.float32
    ).astype(jnp.bfloat16)
    placed = jnp.einsum("at,mad->mtd", select, received, preferred_element_type=jnp.float32)
    kept = jnp.where(region_mask[None, :, None] > 0, jnp.zeros_like(out_store), out_store)
    site_cot = (kept.astype(jnp.float32) + placed).astype(jnp.bfloat16)
    cotangents = jnp.where(section_index == 0, site_cot, out_store)
    onehot = (spins[:, :, None] == jnp.arange(SPINS)[None, None, :]).astype(jnp.bfloat16)
    embed_term = jnp.einsum("mtv,mtd->vd", onehot, site_cot, preferred_element_type=jnp.float32)
    embed_term = jnp.where(section_index == 0, embed_term, jnp.zeros_like(embed_term))
    embed_grad = lax.psum(embed_term, ("samples", "section"))
    return (summed_weight[None], cotangents[None], embed_grad)


NZ = 4
MESH = pl.DeviceIdType.MESH
F32 = jnp.float32
BF = jnp.bfloat16


def dot(a, b, ca=1, cb=0):
    return lax.dot_general(a, b, (((ca,), (cb,)), ((), ())), preferred_element_type=F32)


def kernel(
    x_hbm, g_hbm, w_hbm, layout_hbm, mask_hbm, partner_hbm, spin_hbm,
    wg_ref, cot_ref, emb_ref,
    x_ref, g_ref, layout_ref, mask_ref, partner_ref, spin_ref, gq, w2, pf, pb, rl, rr, att, probs, ga, g0, swz, xsend, xrecv,
    spall, embs, wsend, wrecv, wown,
    in_s, gq_s, gq_r, gf_s, gf_r, w_s, w_r, sp_s, sp_r, at_s, at_r, rs_s, rs_r,
    sw_s, sw_r, xs_s, xs_r, em_s, em_r, wr_s, wr_r,
):
    s = lax.axis_index("samples")
    m = lax.axis_index("mp")
    z = s // 2
    x = s % 2
    scale = 4.0 / HEAD
    tokens, width = x_ref.shape
    heads = width // HEAD
    rows = w_hbm.shape[0]
    half = width // 2
    sibling = {"mp": 1 - m}
    beside = {"samples": 2 * z + 1 - x}

    def rdma(src, dst, ss, rs, dev):
        return pltpu.make_async_remote_copy(
            src_ref=src, dst_ref=dst, send_sem=ss, recv_sem=rs, device_id=dev, device_id_type=MESH
        )

    sends = []

    def send(cond, make):
        if cond is None:
            make().start()
        else:
            pl.when(cond)(lambda: make().start())
        sends.append((cond, make))

    def got(cond, dst, rs):
        def wait():
            rdma(dst, dst, rs, rs, sibling).wait_recv()

        if cond is None:
            wait()
        else:
            pl.when(cond)(wait)

    loads = [
        pltpu.make_async_copy(g_hbm, g_ref, in_s.at[0]),
        pltpu.make_async_copy(w_hbm, w2.at[x], in_s.at[1]),
        pltpu.make_async_copy(x_hbm, x_ref, in_s.at[2]),
        pltpu.make_async_copy(spin_hbm, spin_ref, in_s.at[3]),
        pltpu.make_async_copy(layout_hbm, layout_ref, in_s.at[4]),
        pltpu.make_async_copy(mask_hbm, mask_ref, in_s.at[5]),
        pltpu.make_async_copy(partner_hbm, partner_ref, in_s.at[6]),
    ]
    for load in loads:
        load.start()
    barrier = pltpu.get_barrier_semaphore()
    for k in range(1, 8):
        pl.semaphore_signal(
            barrier, inc=1, device_id={"samples": lax.rem(s + k, 8)}, device_id_type=MESH
        )
    pl.semaphore_signal(barrier, inc=1, device_id=sibling, device_id_type=MESH)
    pl.semaphore_wait(barrier, 8)

    loads[0].wait()
    for j in range(2):
        dz = 2 * m + j
        for_me = dz == z
        piece = g_ref.at[:, pl.ds(j * half, half)]
        send(
            jnp.logical_not(for_me),
            lambda piece=piece, dz=dz, j=j: rdma(
                piece, gq.at[z], gq_s.at[j], gq_r.at[z], {"samples": 2 * dz + x}
            ),
        )
        send(
            for_me,
            lambda piece=piece, j=j: rdma(piece, gq.at[z], gq_s.at[j], gf_r.at[z], sibling),
        )

        @pl.when(for_me)
        def _(j=j):
            gq[z] = g_ref[:, pl.ds(j * half, half)]

    loads[1].wait()
    for c in range(2):
        block = w2.at[x, :, pl.ds(c * half, half)]
        send(None, lambda block=block, c=c: rdma(block, block, w_s.at[c], w_r.at[c], beside))
    loads[3].wait()
    for k in range(1, 8):
        other = lax.rem(s + k, 8)
        send(
            None,
            lambda k=k, other=other: rdma(
                spin_ref, spall.at[s], sp_s.at[k], sp_r.at[s], {"samples": other}
            ),
        )
    spall[s] = spin_ref[...]

    loads[2].wait()
    for load in loads[4:]:
        load.wait()
    qb = lax.broadcasted_iota(jnp.int32, (tokens, tokens), 0) // BLOCK
    kb = lax.broadcasted_iota(jnp.int32, (tokens, tokens), 1) // BLOCK
    linked = jnp.where(qb < kb, layout_ref[0, 1], layout_ref[1, 0])
    allowed = (qb == kb) | (linked > 0)
    for h in range(heads):
        cols = pl.ds(h * HEAD, HEAD)
        xh = x_ref[:, cols]
        scores = jnp.where(allowed, dot(xh, xh, 1, 1) * scale, -jnp.inf)
        expo = jnp.exp(scores - jnp.max(scores, axis=-1, keepdims=True))
        p = expo / jnp.sum(expo, axis=-1, keepdims=True)
        probs[h] = p
        within = pl.ds(h % (heads // 2) * HEAD, HEAD)
        att[h // (heads // 2), z, :, within] = dot(p.astype(BF), xh).astype(BF)

    def hop(buf, ss, rs, c, k):
        send(
            (z < NZ - 1) & (z - k >= 0),
            lambda: rdma(
                buf.at[c, z - k], buf.at[c, z - k], ss.at[0, c, k], rs.at[0, c, k],
                {"samples": s + 2},
            ),
        )
        send(
            (z > 0) & (z + k <= NZ - 1),
            lambda: rdma(
                buf.at[c, z + k], buf.at[c, z + k], ss.at[1, c, k], rs.at[1, c, k],
                {"samples": s - 2},
            ),
        )

    def hop_wait(buf, rs, c, k):
        got(z - 1 - k >= 0, buf.at[c, 0], rs.at[0, c, k])
        got(z + 1 + k <= NZ - 1, buf.at[c, 0], rs.at[1, c, k])

    def att_hop(c, k):
        hop(att, at_s, at_r, c, k)

    def att_wait(c, k):
        hop_wait(att, at_r, c, k)

    att_hop(0, 0)
    att_hop(1, 0)

    first_core = m == z // 2
    for zz in range(NZ):
        near = first_core & (zz != z)
        got(near, gq.at[zz], gq_r.at[zz])
        send(near, lambda zz=zz: rdma(gq.at[zz], gq.at[zz], gf_s.at[zz], gf_r.at[zz], sibling))
    for zz in range(NZ):
        got(jnp.logical_not(first_core), gq.at[zz], gf_r.at[zz])

    def partials(c):
        got(None, w2.at[0, :, pl.ds(c * half, half)], w_r.at[c])
        cols = pl.ds(c * half, half)
        for d in range(NZ):
            part = dot(gq[d, :, :rows], w2[0, :, cols]) + dot(gq[d, :, rows:], w2[1, :, cols])
            pf[c, d] = part
            pb[c, d] = part.astype(BF)

    def end_sends(c, d):
        e = NZ - 1 - d
        send(
            z == NZ - 1,
            lambda: rdma(
                pb.at[c, d], rl.at[c, d], rs_s.at[0, c, d], rs_r.at[0, c, d], {"samples": s - 2}
            ),
        )
        send(
            z == 0,
            lambda: rdma(
                pb.at[c, e], rr.at[c, e], rs_s.at[1, c, e], rs_r.at[1, c, e], {"samples": s + 2}
            ),
        )

    def relay_left(c, at, d):
        here = z == at
        got(here, rl.at[c, d], rs_r.at[0, c, d])

        @pl.when(here)
        def _():
            pb[c, d] = (pf[c, d] + rl[c, d].astype(F32)).astype(BF)

        send(
            here,
            lambda: rdma(
                pb.at[c, d], rl.at[c, d], rs_s.at[0, c, d], rs_r.at[0, c, d], {"samples": s - 2}
            ),
        )

    def relay_right(c, at, e):
        here = z == at
        got(here, rr.at[c, e], rs_r.at[1, c, e])

        @pl.when(here)
        def _():
            pb[c, e] = (pf[c, e] + rr[c, e].astype(F32)).astype(BF)

        send(
            here,
            lambda: rdma(
                pb.at[c, e], rr.at[c, e], rs_s.at[1, c, e], rs_r.at[1, c, e], {"samples": s + 2}
            ),
        )

    def inner(c, d):
        relay_left(c, 2, d)
        relay_right(c, 1, NZ - 1 - d)

    def outer(c):
        relay_left(c, 1, 0)
        relay_right(c, 2, NZ - 1)

    def weight_terms(c):
        for q in range(half // 256):
            cols = pl.ds(c * half + q * 256, 256)
            total = jnp.zeros((2 * rows, 256), F32)
            for zz in range(NZ):
                total += dot(gq[zz], att[c, zz, :, pl.ds(q * 256, 256)], 0, 0).astype(BF).astype(F32)

            @pl.when(x == 0)
            def _(cols=cols, q=q, total=total):
                wown[:, cols] = total[:rows]
                wsend[c, :, pl.ds(q * 256, 256)] = total[rows:].astype(BF)

            @pl.when(x == 1)
            def _(cols=cols, q=q, total=total):
                wown[:, cols] = total[rows:]
                wsend[c, :, pl.ds(q * 256, 256)] = total[:rows].astype(BF)

        send(None, lambda: rdma(wsend.at[c], wrecv.at[c], wr_s.at[c], wr_r.at[c], beside))

    partials(0)
    end_sends(0, 0)
    att_wait(0, 0)
    att_hop(0, 1)
    partials(1)
    end_sends(1, 0)
    for d in range(1, NZ - 1):
        for c in range(2):
            end_sends(c, d)
    inner(0, 0)
    inner(1, 0)
    att_wait(0, 1)
    att_hop(0, 2)
    outer(0)
    inner(0, 1)
    outer(1)
    inner(1, 1)
    att_wait(1, 0)
    att_hop(1, 1)
    att_wait(0, 2)
    weight_terms(0)

    mask = mask_ref[...]
    tri = (
        lax.broadcasted_iota(jnp.int32, (tokens, tokens), 0)
        <= lax.broadcasted_iota(jnp.int32, (tokens, tokens), 1)
    ).astype(F32).astype(BF)
    mask_rows = jnp.broadcast_to(mask, (8, tokens)).astype(F32)
    rank = dot(mask_rows.astype(BF), tri)[:1] - 1.0
    region = tokens // 2
    place = lax.broadcasted_iota(jnp.int32, (region, tokens), 0).astype(F32)
    select = jnp.where((rank == place) & (mask > 0), 1.0, 0.0).astype(BF)

    def backward(c):
        for d in range(NZ - 1):
            got((z == d), rl.at[c, d], rs_r.at[0, c, d])
            got((z == d + 1), rr.at[c, d + 1], rs_r.at[1, c, d + 1])
        for d in range(NZ):

            @pl.when(z == d)
            def _(d=d):
                total = pf[c, d]
                if d < NZ - 1:
                    total += rl[c, d].astype(F32)
                if d > 0:
                    total += rr[c, d].astype(F32)
                ga[...] = total.astype(BF)

        for h in range(heads // 2):
            cols = pl.ds(c * half + h * HEAD, HEAD)
            xh = x_ref[:, cols]
            gh = ga[:, h * HEAD : (h + 1) * HEAD]
            p = probs[c * (heads // 2) + h]
            gp = dot(gh, xh, 1, 1)
            gs = (p * (gp - jnp.sum(gp * p, axis=-1, keepdims=True))).astype(BF)
            through = dot(p.astype(BF), gh, 0, 0) + scale * (dot(gs, xh) + dot(gs, xh, 0, 0))
            g0[:, cols] = (g_ref[:, cols].astype(F32) + through).astype(BF)
        swz[c, z] = dot(select, g0[:, pl.ds(c * half, half)]).astype(BF)
        hop(swz, sw_s, sw_r, c, 0)

    backward(0)
    backward(1)
    att_wait(1, 1)
    att_hop(1, 2)
    for c in range(2):
        hop_wait(swz, sw_r, c, 0)
        hop(swz, sw_s, sw_r, c, 1)

    for k in range(1, 8):
        other = lax.rem(s + k, 8)
        got(None, spall.at[0], sp_r.at[other])
    mine = partner_ref[s]
    spins = jnp.where(mask > 0, spall[mine], spin_ref[...])
    onehot = jnp.where(
        spins == lax.broadcasted_iota(jnp.int32, (8, tokens), 0), 1.0, 0.0
    ).astype(BF)
    embs[s] = dot(onehot, g0[...])[:SPINS]
    for k in range(1, 8):
        other = lax.rem(s + k, 8)
        send(
            None,
            lambda k=k, other=other: rdma(
                embs.at[s], embs.at[s], em_s.at[k], em_r.at[s], {"samples": other}
            ),
        )

    def rows_from(c, which):
        rows_now = swz[c, 0]
        for zz in range(1, NZ):
            rows_now = jnp.where(which == zz, swz[c, zz], rows_now)
        return rows_now

    for c in range(2):
        hop_wait(swz, sw_r, c, 1)
        hop(swz, sw_s, sw_r, c, 2)
    att_wait(1, 2)
    weight_terms(1)
    theirs = partner_ref[2 * z + 1 - x]
    for c in range(2):
        hop_wait(swz, sw_r, c, 2)
        xsend[c] = rows_from(c, theirs // 2)
        send(
            None, lambda c=c: rdma(xsend.at[c], xrecv.at[c], xs_s.at[c], xs_r.at[c], beside)
        )
    same = jnp.where(mine % 2 == x, 1, 0)
    eye = lax.broadcasted_iota(jnp.int32, (tokens, tokens), 0) == lax.broadcasted_iota(
        jnp.int32, (tokens, tokens), 1
    )
    keep = jnp.where(eye & (mask == 0), 1.0, 0.0).astype(BF)
    kept = dot(keep, g0[...])
    for k in range(1, 8):
        got(None, embs.at[0], em_r.at[lax.rem(s + k, 8)])
    total = embs[0]
    for k in range(1, 8):
        total += embs[k]
    emb_ref[...] = total
    for c in range(2):
        cols = slice(c * half, (c + 1) * half)
        got(None, wrecv.at[c], wr_r.at[c])
        wg_ref[:, cols] = wown[:, cols] + wrecv[c].astype(F32)
    for c in range(2):
        cols = slice(c * half, (c + 1) * half)
        got(None, xrecv.at[c], xs_r.at[c])
        chosen = jnp.where(same > 0, rows_from(c, mine // 2), xrecv[c])
        cot_ref[:, cols] = (kept[:, cols] + dot(select, chosen, 0, 0)).astype(BF)

    for cond, make in sends:
        if cond is None:
            make().wait_send()
        else:
            pl.when(cond)(lambda make=make: make().wait_send())


def one_layer(
    stored_inputs, top_cotangent, layer_weights, block_layout, region_mask, partner_samples, spins
):
    tokens, width = stored_inputs.shape[2:]
    rows = layer_weights.shape[1]
    hbm = pl.BlockSpec(memory_space=pltpu.HBM)
    vmem = pl.BlockSpec(memory_space=pltpu.VMEM)
    region = tokens // 2
    dma = pltpu.SemaphoreType.DMA
    half = width // 2
    shapes = [
        ((NZ, tokens, half), BF),
        ((2, rows, width), BF),
        ((2, NZ, tokens, half), F32),
        ((2, NZ, tokens, half), BF),
        ((2, NZ, tokens, half), BF),
        ((2, NZ, tokens, half), BF),
        ((2, NZ, tokens, half), BF),
        ((width // HEAD, tokens, tokens), F32),
        ((tokens, half), BF),
        ((tokens, width), BF),
        ((2, NZ, region, half), BF),
        ((2, region, half), BF),
        ((2, region, half), BF),
        ((8, 1, tokens), jnp.int32),
        ((8, SPINS, width), F32),
        ((2, rows, half), BF),
        ((2, rows, half), BF),
        ((rows, width), F32),
    ]
    sems = [
        dma((7,)), dma((2,)), dma((NZ,)), dma((NZ,)), dma((NZ,)), dma((2,)), dma((2,)),
        dma((8,)), dma((8,)), dma((2, 2, 3)), dma((2, 2, 3)), dma((2, 2, NZ)), dma((2, 2, NZ)),
        dma((2, 2, 3)), dma((2, 2, 3)), dma((2,)), dma((2,)), dma((8,)), dma((8,)), dma((2,)), dma((2,)),
    ]
    wg, cot, emb = pl.pallas_call(
        kernel,
        out_shape=[
            jax.ShapeDtypeStruct((rows, width), F32),
            jax.ShapeDtypeStruct((tokens, width), BF),
            jax.ShapeDtypeStruct((SPINS, width), F32),
        ],
        in_specs=[hbm] * 7,
        out_specs=[vmem] * 3,
        scratch_shapes=[
            pltpu.VMEM((tokens, width), BF),
            pltpu.VMEM((tokens, width), BF),
            pltpu.SMEM((2, 2), jnp.int32),
            pltpu.VMEM((1, tokens), jnp.int32),
            pltpu.SMEM((8,), jnp.int32),
            pltpu.VMEM((1, tokens), jnp.int32),
        ]
        + [pltpu.VMEM(a, b) for a, b in shapes]
        + sems,
        compiler_params=pltpu.CompilerParams(
            collective_id=0, has_side_effects=True, vmem_limit_bytes=64 * 1024 * 1024 - 65536 - 1400 * 1024
        ),
    )(
        stored_inputs[0, 0], top_cotangent[0], layer_weights[0], block_layout[0],
        region_mask[None], partner_samples, spins,
    )
    return wg[None], cot[None, None], emb


def solution(mesh):
    in_specs = (
        P("section", ("groups", "samples"), None, "mp"),
        P(("groups", "samples"), None, "mp"),
        P("section", "samples", "mp"),
        P("section", None, None),
        P(),
        P("groups"),
        P(("groups", "samples"), None),
    )
    out_specs = (
        P(("groups", "section"), "samples", "mp"),
        P("section", ("groups", "samples"), None, "mp"),
        P("groups", "mp"),
    )
    small = mesh.shape["samples"] == 8 and mesh.shape["section"] == 1 and mesh.shape["mp"] == 2
    body = one_layer if small else local
    return jax.shard_map(body, mesh=mesh, in_specs=in_specs, out_specs=out_specs, check_vma=False)
```

```python
import jax
import jax.numpy as jnp
from jax import lax
from jax.experimental import pallas as pl
from jax.experimental.pallas import tpu as pltpu
from jax.sharding import PartitionSpec as P

HEAD = 128
BLOCK = 64
SPINS = 2


def for_sending(value):

    def short(part):
        return part.astype(jnp.bfloat16) if part.dtype == jnp.float32 else part

    return jax.tree.map(short, value)


def passed_along(block, axis, distance):
    devices = range(lax.axis_size(axis))
    route = [(i - distance, i) for i in devices if i - distance in devices]
    return lax.ppermute(block, axis, route)


def softmax_parts(inputs_h, allowed, attention_scale):
    scores = (
        jnp.einsum("qhd,khd->hqk", inputs_h, inputs_h, preferred_element_type=jnp.float32)
        * attention_scale
    )
    scores = jnp.where(allowed[None], scores, -jnp.inf)
    top_score = jnp.max(scores, axis=-1, keepdims=True)
    expo_terms = jnp.exp(scores - top_score)
    probs = expo_terms / jnp.sum(expo_terms, axis=-1, keepdims=True)
    return (probs, probs.astype(jnp.bfloat16))


def local(
    stored_inputs, top_cotangent, layer_weights, block_layout, region_mask, partner_samples, spins
):
    section_index = lax.axis_index("section")
    section_count = lax.axis_size("section")
    micro_count = stored_inputs.shape[1]
    seq_len = stored_inputs.shape[2]
    half_width = stored_inputs.shape[3]
    head_count = half_width // HEAD
    attention_scale = 4.0 / HEAD
    weights = lax.all_gather(layer_weights[0], "samples", axis=0, tiled=True)
    pos_block = jnp.arange(seq_len) // BLOCK
    block_onehot = (pos_block[:, None] == jnp.arange(block_layout.shape[1])[None, :]).astype(
        jnp.float32
    )
    linked = jnp.dot(jnp.dot(block_onehot, block_layout[0].astype(jnp.float32)), block_onehot.T)
    allowed = (linked > 0.5) | (pos_block[:, None] == pos_block[None, :])
    every_layer_input = stored_inputs[0]
    inputs_h = every_layer_input[0].reshape(seq_len, head_count, HEAD)
    probs, probs_low = softmax_parts(inputs_h, allowed, attention_scale)
    attended = jnp.einsum(
        "hqk,khd->qhd", probs_low, inputs_h, preferred_element_type=jnp.float32
    ).astype(jnp.bfloat16)
    probs_list = [probs]
    low_list = [probs_low]
    attend_list = [attended.reshape(seq_len, half_width)]
    probs_all = jnp.stack(probs_list)
    low_all = jnp.stack(low_list)
    attend_store = jnp.stack(attend_list)

    def layer_back(grad_full, grad_own, inputs, probs, probs_low):
        grad_attn = jnp.dot(grad_full, weights, preferred_element_type=jnp.float32).astype(
            jnp.bfloat16
        )
        inputs_h = inputs.reshape(seq_len, head_count, HEAD)
        grad_h = grad_attn.reshape(seq_len, head_count, HEAD)
        grad_probs = jnp.einsum(
            "qhd,khd->hqk", grad_h, inputs_h, preferred_element_type=jnp.float32
        )
        grad_scores = (
            probs * (grad_probs - jnp.sum(grad_probs * probs, axis=-1, keepdims=True))
        ).astype(jnp.bfloat16)
        through = jnp.einsum("hqk,qhd->khd", probs_low, grad_h, preferred_element_type=jnp.float32)
        through = through + attention_scale * (
            jnp.einsum("hqk,khd->qhd", grad_scores, inputs_h, preferred_element_type=jnp.float32)
            + jnp.einsum("hqk,qhd->khd", grad_scores, inputs_h, preferred_element_type=jnp.float32)
        )
        grad_in = grad_own.astype(jnp.float32) + through.reshape(seq_len, half_width)
        return grad_in.astype(jnp.bfloat16)

    def resting(grad_full, grad_own, inputs, probs, probs_low):
        return jnp.zeros((seq_len, half_width), jnp.bfloat16)

    carried_state = jnp.zeros((seq_len, half_width), jnp.bfloat16)
    out_list = []
    grad_list = []
    total_steps = micro_count + section_count - 1
    for step_number in range(total_steps):
        micro_index = step_number - (section_count - 1 - section_index)
        active = (micro_index >= 0) & (micro_index < micro_count)
        slot_index = jnp.clip(micro_index, 0, micro_count - 1)
        from_top = lax.dynamic_index_in_dim(top_cotangent, slot_index, 0, keepdims=False)
        incoming = jnp.where(section_index == section_count - 1, from_top, carried_state)
        grad_full = lax.all_gather(incoming, "mp", axis=1, tiled=True)
        inputs_now = lax.dynamic_index_in_dim(every_layer_input, slot_index, 0, keepdims=False)
        probs_now = lax.dynamic_index_in_dim(probs_all, slot_index, 0, keepdims=False)
        low_now = lax.dynamic_index_in_dim(low_all, slot_index, 0, keepdims=False)
        grad_in = lax.cond(
            active, layer_back, resting, grad_full, incoming, inputs_now, probs_now, low_now
        )
        out_list.append(grad_in)
        grad_list.append(grad_full)
        if step_number < total_steps - 1:
            carried_state = jax.tree.map(
                lambda part, own: part.astype(own.dtype),
                passed_along(for_sending(grad_in), "section", -1),
                grad_in,
            )
    offset = section_count - 1 - section_index
    out_store = lax.dynamic_slice_in_dim(jnp.stack(out_list), offset, micro_count, 0)
    grad_store = lax.dynamic_slice_in_dim(jnp.stack(grad_list), offset, micro_count, 0)
    summed_weight = lax.psum_scatter(
        jnp.einsum(
            "mtf,mta->fa", grad_store, attend_store, preferred_element_type=jnp.float32
        ).astype(jnp.bfloat16),
        "samples",
        scatter_dimension=0,
        tiled=True,
    ).astype(jnp.float32)
    region_count = seq_len // 2
    rank_in_region = jnp.cumsum(region_mask) - 1
    select = (
        (rank_in_region[None, :] == jnp.arange(region_count)[:, None]) & (region_mask[None, :] > 0)
    ).astype(jnp.bfloat16)
    tiles = jnp.einsum("at,mtd->mad", select, out_store, preferred_element_type=jnp.float32).astype(
        jnp.bfloat16
    )
    shard_index = lax.axis_index("samples")
    my_partners = lax.dynamic_slice_in_dim(
        partner_samples, shard_index * micro_count, micro_count, 0
    )
    shard_count = lax.axis_size("samples")
    dest_shard = my_partners // micro_count
    dest_slot = my_partners % micro_count
    route = (
        (dest_shard[:, None, None] == jnp.arange(shard_count)[None, :, None])
        & (dest_slot[:, None, None] == jnp.arange(micro_count)[None, None, :])
    ).astype(jnp.bfloat16)
    outgoing = jnp.einsum("mku,mad->kuad", route, tiles, preferred_element_type=jnp.float32).astype(
        jnp.bfloat16
    )
    arrived = lax.all_to_all(outgoing, "samples", split_axis=0, concat_axis=0, tiled=True)
    ones_row = jnp.ones((shard_count,), jnp.bfloat16)
    received = jnp.einsum(
        "k,kuad->uad", ones_row, arrived, preferred_element_type=jnp.float32
    ).astype(jnp.bfloat16)
    placed = jnp.einsum("at,mad->mtd", select, received, preferred_element_type=jnp.float32)
    kept = jnp.where(region_mask[None, :, None] > 0, jnp.zeros_like(out_store), out_store)
    site_cot = (kept.astype(jnp.float32) + placed).astype(jnp.bfloat16)
    cotangents = jnp.where(section_index == 0, site_cot, out_store)
    onehot = (spins[:, :, None] == jnp.arange(SPINS)[None, None, :]).astype(jnp.bfloat16)
    embed_term = jnp.einsum("mtv,mtd->vd", onehot, site_cot, preferred_element_type=jnp.float32)
    embed_term = jnp.where(section_index == 0, embed_term, jnp.zeros_like(embed_term))
    embed_grad = lax.psum(embed_term, ("samples", "section"))
    return (summed_weight[None], cotangents[None], embed_grad)


NZ = 4
MESH = pl.DeviceIdType.MESH
F32 = jnp.float32
BF = jnp.bfloat16


def dot(a, b, ca=1, cb=0):
    return lax.dot_general(a, b, (((ca,), (cb,)), ((), ())), preferred_element_type=F32)


def kernel(
    x_hbm, g_hbm, w_hbm, layout_hbm, mask_hbm, partner_hbm, spin_hbm,
    wg_ref, cot_ref, emb_ref,
    x_ref, g_ref, layout_ref, mask_ref, partner_ref, spin_ref, gq, w2, pf, pb, rl, rr, att, probs, ga, g0, swz, xsend, xrecv,
    spall, embs, wsend, wrecv, wown,
    in_s, gq_s, gq_r, gf_s, gf_r, w_s, w_r, sp_s, sp_r, at_s, at_r, rs_s, rs_r,
    sw_s, sw_r, xs_s, xs_r, em_s, em_r, wr_s, wr_r,
):
    s = lax.axis_index("samples")
    m = lax.axis_index("mp")
    z = s // 2
    x = s % 2
    scale = 4.0 / HEAD
    tokens, width = x_ref.shape
    heads = width // HEAD
    rows = w_hbm.shape[0]
    half = width // 2
    sibling = {"mp": 1 - m}
    beside = {"samples": 2 * z + 1 - x}

    def rdma(src, dst, ss, rs, dev):
        return pltpu.make_async_remote_copy(
            src_ref=src, dst_ref=dst, send_sem=ss, recv_sem=rs, device_id=dev, device_id_type=MESH
        )

    sends = []

    def send(cond, make):
        if cond is None:
            make().start()
        else:
            pl.when(cond)(lambda: make().start())
        sends.append((cond, make))

    def got(cond, dst, rs):
        def wait():
            rdma(dst, dst, rs, rs, sibling).wait_recv()

        if cond is None:
            wait()
        else:
            pl.when(cond)(wait)

    loads = [
        pltpu.make_async_copy(g_hbm, g_ref, in_s.at[0]),
        pltpu.make_async_copy(w_hbm, w2.at[x], in_s.at[1]),
        pltpu.make_async_copy(x_hbm, x_ref, in_s.at[2]),
        pltpu.make_async_copy(spin_hbm, spin_ref, in_s.at[3]),
        pltpu.make_async_copy(layout_hbm, layout_ref, in_s.at[4]),
        pltpu.make_async_copy(mask_hbm, mask_ref, in_s.at[5]),
        pltpu.make_async_copy(partner_hbm, partner_ref, in_s.at[6]),
    ]
    for load in loads:
        load.start()
    barrier = pltpu.get_barrier_semaphore()
    for k in range(1, 8):
        pl.semaphore_signal(
            barrier, inc=1, device_id={"samples": lax.rem(s + k, 8)}, device_id_type=MESH
        )
    pl.semaphore_signal(barrier, inc=1, device_id=sibling, device_id_type=MESH)
    pl.semaphore_wait(barrier, 8)

    loads[0].wait()
    for j in range(2):
        dz = 2 * m + j
        for_me = dz == z
        piece = g_ref.at[:, pl.ds(j * half, half)]
        send(
            jnp.logical_not(for_me),
            lambda piece=piece, dz=dz, j=j: rdma(
                piece, gq.at[z], gq_s.at[j], gq_r.at[z], {"samples": 2 * dz + x}
            ),
        )
        send(
            for_me,
            lambda piece=piece, j=j: rdma(piece, gq.at[z], gq_s.at[j], gf_r.at[z], sibling),
        )

        @pl.when(for_me)
        def _(j=j):
            gq[z] = g_ref[:, pl.ds(j * half, half)]

    loads[1].wait()
    for c in range(2):
        block = w2.at[x, :, pl.ds(c * half, half)]
        send(None, lambda block=block, c=c: rdma(block, block, w_s.at[c], w_r.at[c], beside))
    loads[3].wait()
    for k in range(1, 8):
        other = lax.rem(s + k, 8)
        send(
            None,
            lambda k=k, other=other: rdma(
                spin_ref, spall.at[s], sp_s.at[k], sp_r.at[s], {"samples": other}
            ),
        )
    spall[s] = spin_ref[...]

    loads[2].wait()
    for load in loads[4:]:
        load.wait()
    qb = lax.broadcasted_iota(jnp.int32, (tokens, tokens), 0) // BLOCK
    kb = lax.broadcasted_iota(jnp.int32, (tokens, tokens), 1) // BLOCK
    linked = jnp.where(qb < kb, layout_ref[0, 1], layout_ref[1, 0])
    allowed = (qb == kb) | (linked > 0)
    for h in range(heads):
        cols = pl.ds(h * HEAD, HEAD)
        xh = x_ref[:, cols]
        scores = jnp.where(allowed, dot(xh, xh, 1, 1) * scale, -jnp.inf)
        expo = jnp.exp(scores - jnp.max(scores, axis=-1, keepdims=True))
        p = expo / jnp.sum(expo, axis=-1, keepdims=True)
        probs[h] = p
        within = pl.ds(h % (heads // 2) * HEAD, HEAD)
        att[h // (heads // 2), z, :, within] = dot(p.astype(BF), xh).astype(BF)

    def hop(buf, ss, rs, c, k):
        send(
            (z < NZ - 1) & (z - k >= 0),
            lambda: rdma(
                buf.at[c, z - k], buf.at[c, z - k], ss.at[0, c, k], rs.at[0, c, k],
                {"samples": s + 2},
            ),
        )
        send(
            (z > 0) & (z + k <= NZ - 1),
            lambda: rdma(
                buf.at[c, z + k], buf.at[c, z + k], ss.at[1, c, k], rs.at[1, c, k],
                {"samples": s - 2},
            ),
        )

    def hop_wait(buf, rs, c, k):
        got(z - 1 - k >= 0, buf.at[c, 0], rs.at[0, c, k])
        got(z + 1 + k <= NZ - 1, buf.at[c, 0], rs.at[1, c, k])

    def att_hop(c, k):
        hop(att, at_s, at_r, c, k)

    def att_wait(c, k):
        hop_wait(att, at_r, c, k)

    att_hop(0, 0)
    att_hop(1, 0)

    first_core = m == z // 2
    for zz in range(NZ):
        near = first_core & (zz != z)
        got(near, gq.at[zz], gq_r.at[zz])
        send(near, lambda zz=zz: rdma(gq.at[zz], gq.at[zz], gf_s.at[zz], gf_r.at[zz], sibling))
    for zz in range(NZ):
        got(jnp.logical_not(first_core), gq.at[zz], gf_r.at[zz])

    def partials(c):
        got(None, w2.at[0, :, pl.ds(c * half, half)], w_r.at[c])
        cols = pl.ds(c * half, half)
        for d in range(NZ):
            part = dot(gq[d, :, :rows], w2[0, :, cols]) + dot(gq[d, :, rows:], w2[1, :, cols])
            pf[c, d] = part
            pb[c, d] = part.astype(BF)

    def end_sends(c, d):
        e = NZ - 1 - d
        send(
            z == NZ - 1,
            lambda: rdma(
                pb.at[c, d], rl.at[c, d], rs_s.at[0, c, d], rs_r.at[0, c, d], {"samples": s - 2}
            ),
        )
        send(
            z == 0,
            lambda: rdma(
                pb.at[c, e], rr.at[c, e], rs_s.at[1, c, e], rs_r.at[1, c, e], {"samples": s + 2}
            ),
        )

    def relay_left(c, at, d):
        here = z == at
        got(here, rl.at[c, d], rs_r.at[0, c, d])

        @pl.when(here)
        def _():
            pb[c, d] = (pf[c, d] + rl[c, d].astype(F32)).astype(BF)

        send(
            here,
            lambda: rdma(
                pb.at[c, d], rl.at[c, d], rs_s.at[0, c, d], rs_r.at[0, c, d], {"samples": s - 2}
            ),
        )

    def relay_right(c, at, e):
        here = z == at
        got(here, rr.at[c, e], rs_r.at[1, c, e])

        @pl.when(here)
        def _():
            pb[c, e] = (pf[c, e] + rr[c, e].astype(F32)).astype(BF)

        send(
            here,
            lambda: rdma(
                pb.at[c, e], rr.at[c, e], rs_s.at[1, c, e], rs_r.at[1, c, e], {"samples": s + 2}
            ),
        )

    def inner(c, d):
        relay_left(c, 2, d)
        relay_right(c, 1, NZ - 1 - d)

    def outer(c):
        relay_left(c, 1, 0)
        relay_right(c, 2, NZ - 1)

    def weight_terms(c):
        for q in range(half // 256):
            cols = pl.ds(c * half + q * 256, 256)
            total = jnp.zeros((2 * rows, 256), F32)
            for zz in range(NZ):
                total += dot(gq[zz], att[c, zz, :, pl.ds(q * 256, 256)], 0, 0).astype(BF).astype(F32)

            @pl.when(x == 0)
            def _(cols=cols, q=q, total=total):
                wown[:, cols] = total[:rows]
                wsend[c, :, pl.ds(q * 256, 256)] = total[rows:].astype(BF)

            @pl.when(x == 1)
            def _(cols=cols, q=q, total=total):
                wown[:, cols] = total[rows:]
                wsend[c, :, pl.ds(q * 256, 256)] = total[:rows].astype(BF)

        send(None, lambda: rdma(wsend.at[c], wrecv.at[c], wr_s.at[c], wr_r.at[c], beside))

    partials(0)
    end_sends(0, 0)
    att_wait(0, 0)
    att_hop(0, 1)
    partials(1)
    end_sends(1, 0)
    for d in range(1, NZ - 1):
        for c in range(2):
            end_sends(c, d)
    inner(0, 0)
    inner(1, 0)
    att_wait(0, 1)
    att_hop(0, 2)
    outer(0)
    inner(0, 1)
    outer(1)
    inner(1, 1)
    att_wait(1, 0)
    att_hop(1, 1)
    att_wait(0, 2)
    weight_terms(0)

    mask = mask_ref[...]
    tri = (
        lax.broadcasted_iota(jnp.int32, (tokens, tokens), 0)
        <= lax.broadcasted_iota(jnp.int32, (tokens, tokens), 1)
    ).astype(F32).astype(BF)
    mask_rows = jnp.broadcast_to(mask, (8, tokens)).astype(F32)
    rank = dot(mask_rows.astype(BF), tri)[:1] - 1.0
    region = tokens // 2
    place = lax.broadcasted_iota(jnp.int32, (region, tokens), 0).astype(F32)
    select = jnp.where((rank == place) & (mask > 0), 1.0, 0.0).astype(BF)

    def backward(c):
        for d in range(NZ - 1):
            got((z == d), rl.at[c, d], rs_r.at[0, c, d])
            got((z == d + 1), rr.at[c, d + 1], rs_r.at[1, c, d + 1])
        for d in range(NZ):

            @pl.when(z == d)
            def _(d=d):
                total = pf[c, d]
                if d < NZ - 1:
                    total += rl[c, d].astype(F32)
                if d > 0:
                    total += rr[c, d].astype(F32)
                ga[...] = total.astype(BF)

        for h in range(heads // 2):
            cols = pl.ds(c * half + h * HEAD, HEAD)
            xh = x_ref[:, cols]
            gh = ga[:, h * HEAD : (h + 1) * HEAD]
            p = probs[c * (heads // 2) + h]
            gp = dot(gh, xh, 1, 1)
            gs = (p * (gp - jnp.sum(gp * p, axis=-1, keepdims=True))).astype(BF)
            through = dot(p.astype(BF), gh, 0, 0) + scale * (dot(gs, xh) + dot(gs, xh, 0, 0))
            g0[:, cols] = (g_ref[:, cols].astype(F32) + through).astype(BF)
        swz[c, z] = dot(select, g0[:, pl.ds(c * half, half)]).astype(BF)
        hop(swz, sw_s, sw_r, c, 0)

    backward(0)
    backward(1)
    att_wait(1, 1)
    att_hop(1, 2)
    for c in range(2):
        hop_wait(swz, sw_r, c, 0)
        hop(swz, sw_s, sw_r, c, 1)

    for k in range(1, 8):
        other = lax.rem(s + k, 8)
        got(None, spall.at[0], sp_r.at[other])
    mine = partner_ref[s]
    spins = jnp.where(mask > 0, spall[mine], spin_ref[...])
    onehot = jnp.where(
        spins == lax.broadcasted_iota(jnp.int32, (8, tokens), 0), 1.0, 0.0
    ).astype(BF)
    embs[s] = dot(onehot, g0[...])[:SPINS]
    for k in range(1, 8):
        other = lax.rem(s + k, 8)
        send(
            None,
            lambda k=k, other=other: rdma(
                embs.at[s], embs.at[s], em_s.at[k], em_r.at[s], {"samples": other}
            ),
        )

    def rows_from(c, which):
        rows_now = swz[c, 0]
        for zz in range(1, NZ):
            rows_now = jnp.where(which == zz, swz[c, zz], rows_now)
        return rows_now

    for c in range(2):
        hop_wait(swz, sw_r, c, 1)
        hop(swz, sw_s, sw_r, c, 2)
    att_wait(1, 2)
    weight_terms(1)
    theirs = partner_ref[2 * z + 1 - x]
    for c in range(2):
        hop_wait(swz, sw_r, c, 2)
        xsend[c] = rows_from(c, theirs // 2)
        send(
            None, lambda c=c: rdma(xsend.at[c], xrecv.at[c], xs_s.at[c], xs_r.at[c], beside)
        )
    same = jnp.where(mine % 2 == x, 1, 0)
    eye = lax.broadcasted_iota(jnp.int32, (tokens, tokens), 0) == lax.broadcasted_iota(
        jnp.int32, (tokens, tokens), 1
    )
    keep = jnp.where(eye & (mask == 0), 1.0, 0.0).astype(BF)
    kept = dot(keep, g0[...])
    for k in range(1, 8):
        got(None, embs.at[0], em_r.at[lax.rem(s + k, 8)])
    total = embs[0]
    for k in range(1, 8):
        total += embs[k]
    emb_ref[...] = total
    for c in range(2):
        cols = slice(c * half, (c + 1) * half)
        got(None, wrecv.at[c], wr_r.at[c])
        wg_ref[:, cols] = wown[:, cols] + wrecv[c].astype(F32)
    for c in range(2):
        cols = slice(c * half, (c + 1) * half)
        got(None, xrecv.at[c], xs_r.at[c])
        chosen = jnp.where(same > 0, rows_from(c, mine // 2), xrecv[c])
        cot_ref[:, cols] = (kept[:, cols] + dot(select, chosen, 0, 0)).astype(BF)

    for cond, make in sends:
        if cond is None:
            make().wait_send()
        else:
            pl.when(cond)(lambda make=make: make().wait_send())


def put_out(wg_ref, cot_ref, emb_ref, wg_out, cot_out, emb_out, done):
    copies = [
        pltpu.make_async_copy(wg_ref, wg_out, done.at[0]),
        pltpu.make_async_copy(cot_ref, cot_out, done.at[1]),
        pltpu.make_async_copy(emb_ref, emb_out, done.at[2]),
    ]
    for copy in copies:
        copy.start()
    for copy in copies:
        copy.wait()


def one_layer(
    stored_inputs, top_cotangent, layer_weights, block_layout, region_mask, partner_samples, spins
):
    tokens, width = stored_inputs.shape[2:]
    rows = layer_weights.shape[1]
    hbm = pl.BlockSpec(memory_space=pltpu.HBM)
    vmem = pl.BlockSpec(memory_space=pltpu.VMEM)
    region = tokens // 2
    dma = pltpu.SemaphoreType.DMA
    half = width // 2
    shapes = [
        ((NZ, tokens, half), BF),
        ((2, rows, width), BF),
        ((2, NZ, tokens, half), F32),
        ((2, NZ, tokens, half), BF),
        ((2, NZ, tokens, half), BF),
        ((2, NZ, tokens, half), BF),
        ((2, NZ, tokens, half), BF),
        ((width // HEAD, tokens, tokens), F32),
        ((tokens, half), BF),
        ((tokens, width), BF),
        ((2, NZ, region, half), BF),
        ((2, region, half), BF),
        ((2, region, half), BF),
        ((8, 1, tokens), jnp.int32),
        ((8, SPINS, width), F32),
        ((2, rows, half), BF),
        ((2, rows, half), BF),
        ((rows, width), F32),
    ]
    sems = [
        dma((7,)), dma((2,)), dma((NZ,)), dma((NZ,)), dma((NZ,)), dma((2,)), dma((2,)),
        dma((8,)), dma((8,)), dma((2, 2, 3)), dma((2, 2, 3)), dma((2, 2, NZ)), dma((2, 2, NZ)),
        dma((2, 2, 3)), dma((2, 2, 3)), dma((2,)), dma((2,)), dma((8,)), dma((8,)), dma((2,)), dma((2,)),
    ]
    wg, cot, emb = pl.pallas_call(
        kernel,
        out_shape=[
            jax.ShapeDtypeStruct((rows, width), F32),
            jax.ShapeDtypeStruct((tokens, width), BF),
            jax.ShapeDtypeStruct((SPINS, width), F32),
        ],
        in_specs=[hbm] * 7,
        out_specs=[vmem] * 3,
        scratch_shapes=[
            pltpu.VMEM((tokens, width), BF),
            pltpu.VMEM((tokens, width), BF),
            pltpu.SMEM((2, 2), jnp.int32),
            pltpu.VMEM((1, tokens), jnp.int32),
            pltpu.SMEM((8,), jnp.int32),
            pltpu.VMEM((1, tokens), jnp.int32),
        ]
        + [pltpu.VMEM(a, b) for a, b in shapes]
        + sems,
        compiler_params=pltpu.CompilerParams(
            collective_id=0, has_side_effects=True, vmem_limit_bytes=48 * 1024 * 1024
        ),
    )(
        *[
            pltpu.with_memory_space_constraint(value, pltpu.HBM)
            for value in (
                stored_inputs[0, 0], top_cotangent[0], layer_weights[0], block_layout[0],
                region_mask[None], partner_samples, spins,
            )
        ]
    )
    anywhere = pl.BlockSpec(memory_space=pl.ANY)
    wg, cot, emb = pl.pallas_call(
        put_out,
        out_shape=[jax.ShapeDtypeStruct(a.shape, a.dtype) for a in (wg, cot, emb)],
        in_specs=[vmem] * 3,
        out_specs=[anywhere] * 3,
        scratch_shapes=[dma((3,))],
        compiler_params=pltpu.CompilerParams(vmem_limit_bytes=8 * 1024 * 1024),
    )(wg, cot, emb)
    return wg[None], cot[None, None], emb


def solution(mesh):
    in_specs = (
        P("section", ("groups", "samples"), None, "mp"),
        P(("groups", "samples"), None, "mp"),
        P("section", "samples", "mp"),
        P("section", None, None),
        P(),
        P("groups"),
        P(("groups", "samples"), None),
    )
    out_specs = (
        P(("groups", "section"), "samples", "mp"),
        P("section", ("groups", "samples"), None, "mp"),
        P("groups", "mp"),
    )
    small = mesh.shape["samples"] == 8 and mesh.shape["section"] == 1 and mesh.shape["mp"] == 2
    body = one_layer if small else local
    return jax.shard_map(body, mesh=mesh, in_specs=in_specs, out_specs=out_specs, check_vma=False)
```
